32 devices in a mesh: parts: 2 (over y), blk: 4 (over z), users: 2 (over x), sub: 2 (over core).
Axes of the slice: x: 2, y: 2, z: 4, core: 2. Of those that a mesh axis runs over, the one named last changes fastest.
Arguments:
- history: bfloat16 [64, 64, 256], P(('parts', 'blk'), 'users'), parts along dimension 0, may hold values from -400 to 400
- lengths: int32 [64], P(('parts', 'blk')), parts along dimension 0, may hold values from 1 to 64
- item_rows: bfloat16 [12288, 512], P(('parts', 'blk', 'users', 'sub')), parts along dimension 0, may hold values from -6 to 6
- w_query: bfloat16 [512, 256], replicated, may hold values from -0.25 to 0.25
- w_item: bfloat16 [512, 256], replicated, may hold values from -0.25 to 0.25
- w_key: bfloat16 [256, 256], replicated, may hold values from -0.375 to 0.375
- w_value: bfloat16 [256, 256], replicated, may hold values from -0.375 to 0.375
- w_pooled: bfloat16 [256, 128], replicated, may hold values from -0.25 to 0.25
- w_joint: bfloat16 [256, 128], replicated, may hold values from -0.25 to 0.25
- bias_hidden: float32 [128], replicated, may hold values from -3 to 3
- w_task: bfloat16 [128, 8], replicated, may hold values from -0.5 to 0.5
- bias_task: float32 [8], replicated, may hold values from -3 to 3
Outputs:
- logits: float32 [64, 9, 8, 1536], P(('parts', 'blk'), None, None, ('users', 'sub')), parts along dimension 0
The draws below stay inside these ranges and needn't reach their ends.
There are 2 independent parts, one for each index of `parts`. The reference program is written for one: setup_inputs(seed, part) draws one part's arguments, and reference() takes and returns one part's arrays. A program takes and returns all parts, laid end to end along the dimension named above; an argument that names none is the same for every part. Nothing has to cross between parts.
All inputs are finite; a program needn't handle non-finite values.
Results may differ from the reference program's by a relative error of at most 0.011.
Values may be sent and summed in bfloat16 or wider, within the bound.
No kernel may reach another device: no remote copies, remote signals or barrier semaphores. Data moves between devices by JAX's collectives and lax.ppermute only.
A program may use at most 64 MiB of HBM per device.

```python
import math
import jax
import jax.numpy as jnp
from jax import lax

DH = 256
DI = 512
HID = 128
TASKS = 8
H = 64
U_DEV = 8
REACH = 4
WIN = 9
USERS = 32
IB = 1536
ITEMS = 6144
N_BLK = 4


def draw_history(key, part):
    entries = jax.random.normal(key, (USERS, H, DH), jnp.float32)
    return jnp.clip(entries, -6.0, 6.0).astype(jnp.bfloat16)


def with_ends(values, rng, low, high):
    shape = values.shape
    place = [jax.random.randint(jax.random.fold_in(rng, axis), (), 0, shape[axis]) for axis in range(len(shape))]
    values = values.at[tuple(place)].set(low)
    longest = shape.index(max(shape))
    place[longest] = (place[longest] + 1) % shape[longest]
    return values.at[tuple(place)].set(high)


def levels(rng, shape, cuts, smallest, largest):
    factor_of, own = 1.0, jax.random.fold_in(rng, 6)
    for dim, shards_of in cuts:
        heights = jnp.exp(jax.random.uniform(jax.random.fold_in(own, dim), (shards_of,), jnp.float32, smallest / len(cuts), largest / len(cuts)))
        factor_of = factor_of * jnp.repeat(heights, shape[dim] // shards_of).reshape([-1 if axis == dim else 1 for axis in range(len(shape))])
    return factor_of


def bell_draw(own_key, shape, width, most, pieces=(), held_as=jnp.bfloat16):
    level = levels(own_key, shape, pieces, -0.22, 0.18) if pieces else 1.0
    values = jax.random.normal(own_key, shape, jnp.float32) * width * level
    return jnp.minimum(jnp.maximum(values, -most), most).astype(held_as)


def setup_inputs(seed: int = 0, part: int = 0) -> dict:
    arg_keys = jax.random.split(jax.random.key(seed), 13)
    part_splits = jax.random.split(jax.random.fold_in(arg_keys[12], part), 13)
    return {
        "history": draw_history(jax.random.fold_in(jax.random.fold_in(arg_keys[12], part), 71), part),
        "lengths": with_ends(jax.random.randint(part_splits[1], (USERS,), 1, H + 1), jax.random.fold_in(part_splits[1], 1), 1, H).astype(jnp.int32),
        "item_rows": bell_draw(part_splits[2], (ITEMS, DI), 1.0, 6.0, ((0, 16),)),
        "w_query": bell_draw(arg_keys[3], (DI, DH), DI ** -0.5, 0.25),
        "w_item": bell_draw(arg_keys[4], (DI, DH), DI ** -0.5, 0.25),
        "w_key": bell_draw(arg_keys[5], (DH, DH), DH ** -0.5, 0.375),
        "w_value": bell_draw(arg_keys[6], (DH, DH), DH ** -0.5, 0.375),
        "w_pooled": bell_draw(arg_keys[7], (DH, HID), (2 * DH) ** -0.5, 0.25),
        "w_joint": bell_draw(arg_keys[8], (DH, HID), (2 * DH) ** -0.5, 0.25),
        "bias_hidden": bell_draw(arg_keys[9], (HID,), 0.5, 3.0, (), jnp.float32),
        "w_task": bell_draw(arg_keys[10], (HID, TASKS), HID ** -0.5, 0.5),
        "bias_task": bell_draw(arg_keys[11], (TASKS,), 0.5, 3.0, (), jnp.float32),
    }


def project(item_rows, w_query, w_item, w_joint, bias_hidden):
    queries = jnp.dot(item_rows, w_query, preferred_element_type=jnp.float32).astype(jnp.bfloat16)
    joined = jnp.dot(item_rows, w_item, preferred_element_type=jnp.float32).astype(jnp.bfloat16)
    item_terms = (jnp.dot(joined, w_joint, preferred_element_type=jnp.float32) + bias_hidden.astype(jnp.float32)).astype(jnp.bfloat16)
    return (queries, item_terms)

def score_pairs(queries, item_terms, key_rows, value_rows, is_valid, w_pooled, w_task, bias_task):
    scale = 1.0 / math.sqrt(queries.shape[-1])
    scores = jnp.einsum('id,utd->uit', queries.astype(jnp.float32), key_rows.astype(jnp.float32)) * scale
    scores = jnp.where(is_valid[:, None, :], scores, -jnp.inf)
    maximum = lax.optimization_barrier(jnp.max(scores, axis=-1, keepdims=True))
    expo = jnp.exp(scores - maximum)
    weights = (expo / lax.optimization_barrier(jnp.sum(expo, axis=-1, keepdims=True))).astype(jnp.bfloat16)
    pooled = jnp.einsum('uit,utd->uid', weights.astype(jnp.float32), value_rows.astype(jnp.float32)).astype(jnp.bfloat16)
    hidden = jnp.einsum('uid,dh->uih', pooled.astype(jnp.float32), w_pooled.astype(jnp.float32)) + item_terms.astype(jnp.float32)[None]
    hidden = jax.nn.relu(hidden).astype(jnp.bfloat16)
    logits = jnp.einsum('uih,hk->uki', hidden.astype(jnp.float32), w_task.astype(jnp.float32))
    return logits + bias_task.astype(jnp.float32)[None, :, None]

def reference(history, lengths, item_rows, w_query, w_item, w_key, w_value, w_pooled, w_joint, bias_hidden, w_task, bias_task):
    queries, item_terms = project(item_rows, w_query, w_item, w_joint, bias_hidden)
    queries = queries.reshape(N_BLK, IB, DH)
    item_terms = item_terms.reshape(N_BLK, IB, HID)
    flat = history.reshape(USERS * H, DH)
    key_rows = jnp.dot(flat, w_key, preferred_element_type=jnp.float32).astype(jnp.bfloat16).reshape(N_BLK, U_DEV, H, DH)
    value_rows = jnp.dot(flat, w_value, preferred_element_type=jnp.float32).astype(jnp.bfloat16).reshape(N_BLK, U_DEV, H, DH)
    is_valid = (jnp.arange(H, dtype=jnp.int32)[None, :] < lengths[:, None]).reshape(N_BLK, U_DEV, H)

    def one_group(index):
        results = []
        for position in range(WIN):
            source = (index + position - REACH) % N_BLK
            results.append(score_pairs(queries[source], item_terms[source], key_rows[index], value_rows[index], is_valid[index], w_pooled, w_task, bias_task))
        return jnp.stack(results, axis=1)
    result = lax.map(one_group, jnp.arange(N_BLK, dtype=jnp.int32))
    return result.reshape(USERS, WIN, TASKS, IB)
```

```python
import functools
import math

import jax
import jax.numpy as jnp
from jax import lax
from jax.experimental import pallas as pl
from jax.experimental.pallas import tpu as pltpu
from jax.sharding import PartitionSpec as P

REACH = 4
WIN = 2 * REACH + 1
LENGTH_ROWS = 16
BF16 = jnp.bfloat16
F32 = jnp.float32
VMEM = pl.BlockSpec(memory_space=pltpu.VMEM)
SMEM = pl.BlockSpec(memory_space=pltpu.SMEM)
ANY = pl.BlockSpec(memory_space=pl.ANY)


def call(kernel, out_shape, in_specs, out_specs, args, flops, scratch=()):
    moved = sum(math.prod(a.shape) * a.dtype.itemsize for a in args)
    return pl.pallas_call(
        kernel,
        out_shape=out_shape,
        in_specs=in_specs,
        out_specs=out_specs,
        scratch_shapes=list(scratch),
        cost_estimate=pl.CostEstimate(flops=flops, bytes_accessed=moved, transcendentals=0),
    )(*args)


def pack_kernel(lengths_ref, history_ref, piece_ref):
    rows, width = piece_ref.shape
    tokens = history_ref.shape[1]
    users = (rows - LENGTH_ROWS) // tokens
    first = lax.axis_index("sub") * users
    piece_ref[: users * tokens, :] = history_ref[pl.ds(first, users)].reshape(users * tokens, width)
    row = lax.broadcasted_iota(jnp.int32, (LENGTH_ROWS, width), 0)
    lengths = jnp.zeros((LENGTH_ROWS, width), F32)
    for user in range(users):
        lengths = jnp.where(row == user, lengths_ref[first + user].astype(F32), lengths)
    piece_ref[users * tokens :, :] = lengths.astype(BF16)


def project_kernel(items_ref, w_query_ref, w_item_ref, w_joint_ref, bias_ref, out_ref):
    width = w_query_ref.shape[1]
    rows = items_ref[...]
    queries = jnp.dot(rows, w_query_ref[...], preferred_element_type=F32)
    out_ref[:width, :] = queries.T.astype(BF16)
    joined = jnp.dot(rows, w_item_ref[...], preferred_element_type=F32).astype(BF16)
    terms = jnp.dot(joined, w_joint_ref[...], preferred_element_type=F32) + bias_ref[...]
    out_ref[width:, :] = terms.T.astype(BF16)


def keys_values(pieces, w_key_ref, w_value_ref, w_pooled_ref, key_ref, pooled_ref, mask_ref, turn):
    users, count, width = key_ref.shape
    share = users // len(pieces)
    w_pooled = w_pooled_ref[...].astype(F32).T.astype(BF16)
    for s, parts in enumerate(pieces):
        tokens = count // len(parts)
        lengths = turn[s]
        for r, (rows, first) in enumerate(parts):
            keys = jnp.dot(rows, w_key_ref[...], preferred_element_type=F32).astype(BF16)
            values = jnp.dot(rows, w_value_ref[...], preferred_element_type=F32).astype(BF16)
            place = slice(r * tokens, (r + 1) * tokens)
            at = lax.broadcasted_iota(jnp.int32, (tokens, 128), 0) + first
            at = at.astype(F32)
            for u in range(share):
                user = s * share + u
                key_ref[user, place, :] = keys[u * tokens : (u + 1) * tokens]
                pooled = lax.dot_general(
                    w_pooled,
                    values[u * tokens : (u + 1) * tokens],
                    (((1,), (1,)), ((), ())),
                    preferred_element_type=F32,
                )
                pooled_ref[user, :, place] = pooled.astype(BF16)
                mask_ref[user, place, :] = jnp.where(at < lengths[u : u + 1, :128], 0.0, -jnp.inf)


def score(items_ref, key_ref, pooled_ref, mask_ref, w_task_ref, bias_task_ref, out_ref, shares):
    users, _, width = key_ref.shape
    tasks = w_task_ref.shape[1]
    hid = w_task_ref.shape[0]
    share = users // shares
    factor = math.log2(math.e) / math.sqrt(width)
    queries = items_ref[:width, :]
    terms = items_ref[width:, :].astype(F32)
    columns = terms.shape[1]
    w_task = w_task_ref[...].astype(F32).T
    blank = jnp.zeros_like(w_task)
    heads = jnp.concatenate(
        [jnp.concatenate([w_task, blank], 1), jnp.concatenate([blank, w_task], 1)], 0
    ).astype(BF16)
    row = lax.broadcasted_iota(jnp.int32, (2 * tasks, columns), 0)
    bias = jnp.zeros((2 * tasks, columns), F32)
    for task in range(tasks):
        bias = jnp.where(row % tasks == task, bias_task_ref[task], bias)

    def hidden(user):
        scores = jnp.dot(key_ref[user], queries, preferred_element_type=F32)
        mask = mask_ref[user]
        scores = scores + jnp.concatenate([mask] * (columns // 128), 1)
        maximum = jnp.max(scores, axis=0, keepdims=True)
        expo = jnp.exp2((scores - maximum) * factor)
        weights = (expo * (1.0 / jnp.sum(expo, axis=0, keepdims=True))).astype(BF16)
        total = jnp.dot(pooled_ref[user], weights, preferred_element_type=F32) + terms
        return jnp.maximum(total, 0.0).astype(BF16)

    for s in range(shares):
        first = lax.rem(lax.axis_index("sub") + s, shares) * share
        for u in range(0, share, 2):
            both = jnp.concatenate([hidden(s * share + u), hidden(s * share + u + 1)], 0)
            logits = jnp.dot(heads, both, preferred_element_type=F32) + bias
            if len(out_ref.shape) == 3:
                out_ref[first + u] = logits[:tasks]
                out_ref[first + u + 1] = logits[tasks:]
            else:
                place = pl.multiple_of((first + u) * tasks, 2 * tasks)
                out_ref[pl.ds(place, 2 * tasks), :] = logits.astype(out_ref.dtype)


def first_kernel(own, shares, parts, *refs):
    if own:
        history_ref, refs = refs[0], refs[1:]
    given = [own and s > 0 and r == 0 and parts > 1 for s in range(shares) for r in range(parts)]
    count = given.count(False)
    sent, refs = list(refs[:count]), refs[count:]
    piece_refs = [None if local else sent.pop(0) for local in given]
    w_key_ref, w_value_ref, w_pooled_ref, items_ref, w_task_ref, bias_task_ref = refs[:6]
    out_ref, key_ref, pooled_ref, mask_ref = refs[6:]
    me, side = lax.axis_index("users"), lax.axis_index("sub")
    pieces, turn = [], []
    rows = piece_refs[0].shape[0] - LENGTH_ROWS
    for s in range(shares):
        entries = []
        for r in range(parts):
            ref = piece_refs[s * parts + r]
            if own and s > 0 and r == 0:
                users = history_ref.shape[0] // shares
                chosen = history_ref[pl.ds(lax.rem(side + s, shares) * users, users)]
                content = chosen.reshape(rows, history_ref.shape[2])
            else:
                content = ref[:rows, :]
            tokens = key_ref.shape[1] // parts
            entries.append((content, lax.rem(me + r, parts) * tokens))
        pieces.append(entries)
        turn.append(piece_refs[s * parts + parts - 1][rows:, :].astype(F32))
    keys_values(pieces, w_key_ref, w_value_ref, w_pooled_ref, key_ref, pooled_ref, mask_ref, turn)
    score(items_ref, key_ref, pooled_ref, mask_ref, w_task_ref, bias_task_ref, out_ref, shares)


def next_kernel(shares, items_ref, key_ref, pooled_ref, mask_ref, w_task_ref, bias_task_ref, out_ref):
    score(items_ref, key_ref, pooled_ref, mask_ref, w_task_ref, bias_task_ref, out_ref, shares)


def place_kernel(count, *refs):
    own_refs, away_refs, (out_ref, held, sems) = refs[:2], refs[2:count], refs[count:]
    users, _, tasks, _ = out_ref.shape
    me = lax.axis_index("blk")
    copies = []
    for at, ref in enumerate(own_refs):
        held[at] = ref[...]
    for at, ref in enumerate(away_refs):
        for user in range(0, users, 2):
            both = ref[user * tasks : (user + 2) * tasks, :].astype(F32)
            held[at + 2, user] = both[:tasks]
            held[at + 2, user + 1] = both[tasks:]
    for position in range(WIN):
        block = lax.rem(me + (position - REACH) % count, count)
        ahead = lax.rem(block // 2 - me // 2 + count // 2, count // 2)
        source = 2 * ahead + lax.rem(block + me, 2)
        copy = pltpu.make_async_copy(held.at[source], out_ref.at[:, position], sems.at[position])
        copy.start()
        copies.append(copy)
    for copy in copies:
        copy.wait()


def shift(block, axis, distance):
    count = lax.axis_size(axis)
    return lax.ppermute(block, axis, [((i + distance) % count, i) for i in range(count)])


def from_pair(block, distance):
    count = lax.axis_size("blk")
    return lax.ppermute(block, "blk", [((i + 2 * distance) % count, i) for i in range(count)])


def spread(piece, shares, parts, own=False):
    row = [piece] + [shift(piece, "users", r) for r in range(1, parts)]
    table = [row]
    for s in range(1, shares):
        away = [shift(entry, "sub", s) for entry in row[1:]]
        table.append([None if own and parts > 1 else shift(piece, "sub", s)] + away)
    return table


def shards(
    history,
    lengths,
    item_rows,
    w_query,
    w_item,
    w_key,
    w_value,
    w_pooled,
    w_joint,
    bias_hidden,
    w_task,
    bias_task,
):
    users, tokens, width = history.shape
    items = item_rows.shape[0]
    hid, tasks = w_task.shape
    count, parts, shares = (lax.axis_size(axis) for axis in ("blk", "users", "sub"))
    full = tokens * parts

    piece = call(
        pack_kernel,
        jax.ShapeDtypeStruct((users // shares * tokens + LENGTH_ROWS, width), BF16),
        [SMEM, VMEM],
        VMEM,
        (lengths, history),
        0,
    )
    mine = call(
        project_kernel,
        jax.ShapeDtypeStruct((width + hid, items), BF16),
        [VMEM] * 5,
        VMEM,
        (item_rows, w_query, w_item, w_joint, bias_hidden[None]),
        2 * items * item_rows.shape[1] * 2 * width,
    )
    flops = 2 * users * items * (full * (width + hid) + hid * tasks)
    state = (
        jax.ShapeDtypeStruct((users, full, width), BF16),
        jax.ShapeDtypeStruct((users, hid, full), BF16),
        jax.ShapeDtypeStruct((users, full, 128), F32),
    )
    kept = jax.ShapeDtypeStruct((users, tasks, items), F32)
    sent = jax.ShapeDtypeStruct((users * tasks, items), BF16)

    def start(table, block, out, own):
        flat = [entry for row in table for entry in row if entry is not None]
        head = [history] if own else []
        result = call(
            functools.partial(first_kernel, own, shares, parts),
            (out, *state),
            [VMEM] * (len(head) + len(flat) + 5) + [SMEM],
            [VMEM] * 4,
            (*head, *flat, w_key, w_value, w_pooled, block, w_task, bias_task),
            flops + 4 * users * full * width * width,
        )
        return result[0], result[1:]

    def go_on(held, block, out):
        return call(
            functools.partial(next_kernel, shares),
            out,
            [VMEM] * 5 + [SMEM],
            VMEM,
            (block, *held, w_task, bias_task),
            flops,
        )

    if count % 2 or count > WIN:
        window = [None] * WIN
        window[REACH], held = start(spread(piece, shares, parts, True), mine, kept, True)
        low = high = mine
        for offset in range(1, REACH + 1):
            low, high = shift(low, "blk", -1), shift(high, "blk", 1)
            window[REACH - offset] = go_on(held, low, kept)
            window[REACH + offset] = go_on(held, high, kept)
        return jnp.stack(window, axis=1)

    far = [from_pair(piece, ahead) for ahead in range(1, count // 2)]
    own = spread(piece, shares, parts, True)
    other = lax.ppermute(mine, "blk", [(i ^ 1, i) for i in range(count)])
    at_home, held = start(own, mine, kept, True)
    away = []
    for ahead, entry in enumerate(far, 1):
        near, guests = start(spread(entry, shares, parts), mine, sent, False)
        back = [from_pair(near, -ahead)]
        back.append(from_pair(go_on(guests, other, sent), -ahead))
        away.append(back)
    beside = go_on(held, other, kept)
    results = [entry for back in reversed(away) for entry in back]
    return call(
        functools.partial(place_kernel, count),
        jax.ShapeDtypeStruct((users, WIN, tasks, items), F32),
        [VMEM] * count,
        ANY,
        (at_home, beside, *results),
        0,
        (pltpu.VMEM((count, users, tasks, items), F32), pltpu.SemaphoreType.DMA((WIN,))),
    )


def solution(mesh):
    placed = (
        P(("parts", "blk"), "users", None),
        P(("parts", "blk")),
        P(("parts", "blk", "users", "sub"), None),
        P(),
        P(),
        P(),
        P(),
        P(),
        P(),
        P(),
        P(),
        P(),
    )
    return jax.shard_map(
        shards,
        mesh=mesh,
        in_specs=placed,
        out_specs=P(("parts", "blk"), None, None, ("users", "sub")),
        check_vma=False,
    )
```

```python
import functools
import math

import jax
import jax.numpy as jnp
from jax import lax
from jax.experimental import pallas as pl
from jax.experimental.pallas import tpu as pltpu
from jax.sharding import PartitionSpec as P

REACH = 4
WIN = 2 * REACH + 1
LENGTH_ROWS = 16
BF16 = jnp.bfloat16
F32 = jnp.float32
VMEM = pl.BlockSpec(memory_space=pltpu.VMEM)
SMEM = pl.BlockSpec(memory_space=pltpu.SMEM)
ANY = pl.BlockSpec(memory_space=pl.ANY)


def near(array):
    return pltpu.with_memory_space_constraint(array, pltpu.VMEM)


def call(kernel, out_shape, in_specs, out_specs, args, flops, scratch=()):
    moved = sum(math.prod(a.shape) * a.dtype.itemsize for a in args)
    args = [near(a) if spec is VMEM else a for a, spec in zip(args, in_specs)]
    return pl.pallas_call(
        kernel,
        out_shape=out_shape,
        in_specs=in_specs,
        out_specs=out_specs,
        scratch_shapes=list(scratch),
        cost_estimate=pl.CostEstimate(flops=flops, bytes_accessed=moved, transcendentals=0),
    )(*args)


def pack_kernel(lengths_ref, history_ref, piece_ref):
    rows, width = piece_ref.shape
    tokens = history_ref.shape[1]
    users = (rows - LENGTH_ROWS) // tokens
    first = lax.axis_index("sub") * users
    piece_ref[: users * tokens, :] = history_ref[pl.ds(first, users)].reshape(users * tokens, width)
    row = lax.broadcasted_iota(jnp.int32, (LENGTH_ROWS, width), 0)
    lengths = jnp.zeros((LENGTH_ROWS, width), F32)
    for user in range(users):
        lengths = jnp.where(row == user, lengths_ref[first + user].astype(F32), lengths)
    piece_ref[users * tokens :, :] = lengths.astype(BF16)


def project_kernel(items_ref, w_query_ref, w_item_ref, w_joint_ref, bias_ref, out_ref):
    width = w_query_ref.shape[1]
    rows = items_ref[...]
    queries = jnp.dot(rows, w_query_ref[...], preferred_element_type=F32)
    out_ref[:width, :] = queries.T.astype(BF16)
    joined = jnp.dot(rows, w_item_ref[...], preferred_element_type=F32).astype(BF16)
    terms = jnp.dot(joined, w_joint_ref[...], preferred_element_type=F32) + bias_ref[...]
    out_ref[width:, :] = terms.T.astype(BF16)


def keys_values(pieces, turn, w_key_ref, w_value_ref, w_pooled_ref, key_ref, pooled_ref, mask_ref, history_ref):
    pairs, _, both = pooled_ref.shape
    full = both // 2
    users = 2 * pairs
    share = users // len(pieces)
    for s, parts in enumerate(pieces):
        tokens = full // len(parts)
        for r, (rows, first) in enumerate(parts):
            at = (lax.broadcasted_iota(jnp.int32, (tokens, 128), 0) + first).astype(F32)
            for u in range(share):
                start = (s * share + u) * full + r * tokens
                place = slice(start, start + tokens)
                history_ref[place, :] = rows[u * tokens : (u + 1) * tokens]
                mask_ref[place, :] = jnp.where(at < turn[s][u : u + 1, :128], 0.0, -jnp.inf)
    key_ref[...] = jnp.dot(history_ref[...], w_key_ref[...], preferred_element_type=F32).astype(BF16)
    values = jnp.dot(history_ref[...], w_value_ref[...], preferred_element_type=F32).astype(BF16)
    pooled = jnp.dot(values, w_pooled_ref[...], preferred_element_type=F32)
    hid = pooled.shape[1]
    lane = lax.broadcasted_iota(jnp.int32, (hid, both), 1)
    for pair in range(pairs):
        flat = pooled[pair * both : (pair + 1) * both].T
        pooled_ref[pair, :hid, :] = jnp.where(lane < full, flat, 0.0).astype(BF16)
        pooled_ref[pair, hid:, :] = jnp.where(lane < full, 0.0, flat).astype(BF16)


def score(items_ref, state, w_task_ref, bias_task_ref, out_ref, scratch, shares):
    key_ref, pooled_ref, mask_ref = state
    scores_ref, weights_ref, hidden_ref = scratch
    width = key_ref.shape[1]
    tasks, hid = w_task_ref.shape
    pairs, _, both = pooled_ref.shape
    full = both // 2
    share = pairs // shares
    columns = items_ref.shape[1]
    factor = math.log2(math.e) / math.sqrt(width)
    w_task = w_task_ref[...].astype(F32)
    blank = jnp.zeros_like(w_task)
    heads = jnp.concatenate(
        [jnp.concatenate([w_task, blank], 1), jnp.concatenate([blank, w_task], 1)], 0
    ).astype(BF16)
    row = lax.broadcasted_iota(jnp.int32, (2 * tasks, columns), 0)
    bias = jnp.zeros((2 * tasks, columns), F32)
    for task in range(tasks):
        bias = jnp.where(row % tasks == task, bias_task_ref[task], bias)

    scores_ref[...] = jnp.dot(key_ref[...], items_ref[:width, :], preferred_element_type=F32)
    for user in range(2 * pairs):
        rows = slice(user * full, (user + 1) * full)
        for column in range(0, columns, 128):
            lanes = slice(column, column + 128)
            scores = scores_ref[rows, lanes] + mask_ref[rows, :]
            maximum = jnp.max(scores, axis=0, keepdims=True)
            expo = jnp.exp2((scores - maximum) * factor)
            weights = expo * (1.0 / jnp.sum(expo, axis=0, keepdims=True))
            weights_ref[rows, lanes] = weights.astype(BF16)
    for pair in range(pairs):
        rows = slice(pair * both, (pair + 1) * both)
        total = jnp.dot(pooled_ref[pair], weights_ref[rows, :], preferred_element_type=F32)
        for user in range(2):
            part = slice(user * hid, (user + 1) * hid)
            hidden = total[part] + items_ref[width:, :].astype(F32)
            hidden_ref[pair, part, :] = jnp.maximum(hidden, 0.0).astype(BF16)
    for pair in range(pairs):
        logits = jnp.dot(heads, hidden_ref[pair], preferred_element_type=F32) + bias
        first = lax.rem(lax.axis_index("sub") + pair // share, shares) * share + pair % share
        if len(out_ref.shape) == 3:
            out_ref[2 * first] = logits[:tasks]
            out_ref[2 * first + 1] = logits[tasks:]
        else:
            place = pl.multiple_of(2 * first * tasks, 2 * tasks)
            out_ref[pl.ds(place, 2 * tasks), :] = logits.astype(out_ref.dtype)


def first_kernel(own, shares, parts, *refs):
    if own:
        history_ref, refs = refs[0], refs[1:]
    given = [own and s > 0 and r == 0 and parts > 1 for s in range(shares) for r in range(parts)]
    count = given.count(False)
    sent, refs = list(refs[:count]), refs[count:]
    piece_refs = [None if local else sent.pop(0) for local in given]
    w_key_ref, w_value_ref, w_pooled_ref, items_ref, w_task_ref, bias_task_ref = refs[:6]
    out_ref, key_ref, pooled_ref, mask_ref, rows_ref, *scratch = refs[6:]
    me, side = lax.axis_index("users"), lax.axis_index("sub")
    pieces, turn = [], []
    rows = piece_refs[0].shape[0] - LENGTH_ROWS
    tokens = pooled_ref.shape[2] // 2 // parts
    for s in range(shares):
        entries = []
        for r in range(parts):
            ref = piece_refs[s * parts + r]
            if own and s > 0 and r == 0:
                users = history_ref.shape[0] // shares
                chosen = history_ref[pl.ds(lax.rem(side + s, shares) * users, users)]
                content = chosen.reshape(rows, history_ref.shape[2])
            else:
                content = ref[:rows, :]
            entries.append((content, lax.rem(me + r, parts) * tokens))
        pieces.append(entries)
        turn.append(piece_refs[s * parts + parts - 1][rows:, :].astype(F32))
    state = (key_ref, pooled_ref, mask_ref)
    keys_values(pieces, turn, w_key_ref, w_value_ref, w_pooled_ref, *state, rows_ref)
    score(items_ref, state, w_task_ref, bias_task_ref, out_ref, scratch, shares)


def next_kernel(shares, items_ref, key_ref, pooled_ref, mask_ref, w_task_ref, bias_task_ref, out_ref, *scratch):
    state = (key_ref, pooled_ref, mask_ref)
    score(items_ref, state, w_task_ref, bias_task_ref, out_ref, scratch, shares)


def place_kernel(count, *refs):
    own_refs, away_refs, (out_ref, held, sems) = refs[:2], refs[2:count], refs[count:]
    users, _, tasks, _ = out_ref.shape
    me = lax.axis_index("blk")
    copies = []
    for at, ref in enumerate(own_refs):
        held[at] = ref[...]
    for at, ref in enumerate(away_refs):
        for user in range(0, users, 2):
            both = ref[user * tasks : (user + 2) * tasks, :].astype(F32)
            held[at + 2, user] = both[:tasks]
            held[at + 2, user + 1] = both[tasks:]
    for position in range(WIN):
        block = lax.rem(me + (position - REACH) % count, count)
        ahead = lax.rem(block // 2 - me // 2 + count // 2, count // 2)
        source = 2 * ahead + lax.rem(block + me, 2)
        copy = pltpu.make_async_copy(held.at[source], out_ref.at[:, position], sems.at[position])
        copy.start()
        copies.append(copy)
    for copy in copies:
        copy.wait()


def shift(block, axis, distance):
    count = lax.axis_size(axis)
    return lax.ppermute(block, axis, [((i + distance) % count, i) for i in range(count)])


def from_pair(block, distance):
    count = lax.axis_size("blk")
    return lax.ppermute(block, "blk", [((i + 2 * distance) % count, i) for i in range(count)])


def spread(piece, shares, parts, own=False):
    row = [piece] + [shift(piece, "users", r) for r in range(1, parts)]
    table = [row]
    for s in range(1, shares):
        away = [shift(entry, "sub", s) for entry in row[1:]]
        table.append([None if own and parts > 1 else shift(piece, "sub", s)] + away)
    return table


def shards(
    history,
    lengths,
    item_rows,
    w_query,
    w_item,
    w_key,
    w_value,
    w_pooled,
    w_joint,
    bias_hidden,
    w_task,
    bias_task,
):
    users, tokens, width = history.shape
    items = item_rows.shape[0]
    hid, tasks = w_task.shape
    count, parts, shares = (lax.axis_size(axis) for axis in ("blk", "users", "sub"))
    full = tokens * parts

    piece = call(
        pack_kernel,
        pltpu.VMEM((users // shares * tokens + LENGTH_ROWS, width), BF16),
        [SMEM, VMEM],
        VMEM,
        (lengths, history),
        0,
    )
    mine = call(
        project_kernel,
        pltpu.VMEM((width + hid, items), BF16),
        [VMEM] * 5,
        VMEM,
        (item_rows, w_query, w_item, w_joint, bias_hidden[None]),
        2 * items * item_rows.shape[1] * 2 * width,
    )
    flops = 2 * users * items * (full * (width + hid) + hid * tasks)
    state = (
        pltpu.VMEM((users * full, width), BF16),
        pltpu.VMEM((users // 2, 2 * hid, 2 * full), BF16),
        pltpu.VMEM((users * full, 128), F32),
    )
    kept = pltpu.VMEM((users, tasks, items), F32)
    sent = pltpu.VMEM((users * tasks, items), BF16)
    scratch = (
        pltpu.VMEM((users * full, items), F32),
        pltpu.VMEM((users * full, items), BF16),
        pltpu.VMEM((users // 2, 2 * hid, items), BF16),
    )

    def start(table, block, out, own):
        flat = [entry for row in table for entry in row if entry is not None]
        head = [history] if own else []
        result = call(
            functools.partial(first_kernel, own, shares, parts),
            (out, *state),
            [VMEM] * (len(head) + len(flat) + 5) + [SMEM],
            [VMEM] * 4,
            (*head, *flat, w_key, w_value, w_pooled, block, w_task.T, bias_task),
            flops + 4 * users * full * width * width,
            (pltpu.VMEM((users * full, width), BF16), *scratch),
        )
        return result[0], result[1:]

    def go_on(held, block, out):
        return call(
            functools.partial(next_kernel, shares),
            out,
            [VMEM] * 5 + [SMEM],
            VMEM,
            (block, *held, w_task.T, bias_task),
            flops,
            scratch,
        )

    if count % 2 or count > WIN:
        window = [None] * WIN
        window[REACH], held = start(spread(piece, shares, parts, True), mine, kept, True)
        low = high = mine
        for offset in range(1, REACH + 1):
            low, high = shift(low, "blk", -1), shift(high, "blk", 1)
            window[REACH - offset] = go_on(held, low, kept)
            window[REACH + offset] = go_on(held, high, kept)
        return jnp.stack(window, axis=1)

    far = [from_pair(piece, ahead) for ahead in range(1, count // 2)]
    own = spread(piece, shares, parts, True)
    other = lax.ppermute(mine, "blk", [(i ^ 1, i) for i in range(count)])
    at_home, held = start(own, mine, kept, True)
    away = []
    for ahead, entry in enumerate(far, 1):
        result, guests = start(spread(entry, shares, parts), mine, sent, False)
        back = [from_pair(result, -ahead)]
        back.append(from_pair(go_on(guests, other, sent), -ahead))
        away.append(back)
    beside = go_on(held, other, kept)
    results = [entry for back in reversed(away) for entry in back]
    return call(
        functools.partial(place_kernel, count),
        jax.ShapeDtypeStruct((users, WIN, tasks, items), F32),
        [VMEM] * count,
        ANY,
        (at_home, beside, *results),
        0,
        (pltpu.VMEM((count, users, tasks, items), F32), pltpu.SemaphoreType.DMA((WIN,))),
    )


def solution(mesh):
    placed = (
        P(("parts", "blk"), "users", None),
        P(("parts", "blk")),
        P(("parts", "blk", "users", "sub"), None),
        P(),
        P(),
        P(),
        P(),
        P(),
        P(),
        P(),
        P(),
        P(),
    )
    return jax.shard_map(
        shards,
        mesh=mesh,
        in_specs=placed,
        out_specs=P(("parts", "blk"), None, None, ("users", "sub")),
        check_vma=False,
    )
```

```python
import functools
import math

import jax
import jax.numpy as jnp
from jax import lax
from jax.experimental import pallas as pl
from jax.experimental.pallas import tpu as pltpu
from jax.sharding import PartitionSpec as P


REACH = 4
WIN = 2 * REACH + 1
LENGTH_ROWS = 16
KERNEL_BYTES = 16 << 20
BF16 = jnp.bfloat16
F32 = jnp.float32
VMEM = pl.BlockSpec(memory_space=pltpu.VMEM)
SMEM = pl.BlockSpec(memory_space=pltpu.SMEM)
HBM = pl.BlockSpec(memory_space=pltpu.HBM)


def near(array):
    return pltpu.with_memory_space_constraint(array, pltpu.VMEM)


def call(kernel, out_shape, in_specs, out_specs, args, flops, scratch=()):
    moved = sum(math.prod(a.shape) * a.dtype.itemsize for a in args)
    args = [near(a) if spec is VMEM else a for a, spec in zip(args, in_specs)]
    return pl.pallas_call(
        kernel,
        out_shape=out_shape,
        in_specs=in_specs,
        out_specs=out_specs,
        scratch_shapes=list(scratch),
        compiler_params=pltpu.CompilerParams(vmem_limit_bytes=KERNEL_BYTES),
        cost_estimate=pl.CostEstimate(flops=flops, bytes_accessed=moved, transcendentals=0),
    )(*args)


def prepare_kernel(shares, *refs):
    sources, outs, scratch = refs[:9], refs[9:13], refs[13:]
    history_ref, sources = sources[0], sources[1:]
    piece_ref, items_out, heads_ref, bias_out = outs
    held, sems, token_sem = scratch[:8], scratch[8], scratch[9]
    copies = [pltpu.make_async_copy(*pair, sems.at[i]) for i, pair in enumerate(zip(sources, held))]
    users, tokens, _ = history_ref.shape
    users //= shares
    first = lax.axis_index("sub") * users
    width = piece_ref.shape[1]
    moves = []
    for user in range(users):
        place = piece_ref.at[pl.ds(user * tokens, tokens)]
        moves.append(pltpu.make_async_copy(history_ref.at[first + user], place, token_sem.at[user]))
    for copy in copies + moves:
        copy.start()
    rows_ref, w_query_ref, w_item_ref, w_joint_ref, bias_ref, w_task_ref, bias_task_ref, lengths_ref = held

    for copy in copies[5:]:
        copy.wait()
    row = lax.broadcasted_iota(jnp.int32, (LENGTH_ROWS, width), 0)
    lengths = jnp.zeros((LENGTH_ROWS, width), F32)
    for user in range(users):
        lengths = jnp.where(row == user, lengths_ref[first + user].astype(F32), lengths)
    piece_ref[users * tokens :, :] = lengths.astype(BF16)
    tasks, hid = w_task_ref.shape
    w_task = w_task_ref[...].astype(F32)
    blank = jnp.zeros_like(w_task)
    heads_ref[:, :hid] = jnp.concatenate([w_task, blank], 0).astype(BF16)
    heads_ref[:, hid:] = jnp.concatenate([blank, w_task], 0).astype(BF16)
    row = lax.broadcasted_iota(jnp.int32, bias_out.shape, 0) % tasks
    bias = jnp.zeros(bias_out.shape, F32)
    for task in range(tasks):
        bias = jnp.where(row == task, bias_task_ref[task], bias)
    bias_out[...] = bias

    for copy in copies[:5]:
        copy.wait()
    rows = rows_ref[...]
    queries = jnp.dot(rows, w_query_ref[...], preferred_element_type=F32)
    items_out[:width, :] = queries.T.astype(BF16)
    joined = jnp.dot(rows, w_item_ref[...], preferred_element_type=F32).astype(BF16)
    terms = jnp.dot(joined, w_joint_ref[...], preferred_element_type=F32) + bias_ref[...]
    items_out[width:, :] = terms.T.astype(BF16)
    for move in moves:
        move.wait()


def keys_values(pieces, turn, w_key_ref, w_value_ref, w_pooled_ref, key_ref, pooled_ref, mask_ref, history_ref):
    pairs, hid, depth = pooled_ref.shape
    hid //= 2
    both = depth - hid
    full = both // 2
    users = 2 * pairs
    share = users // len(pieces)
    for s, parts in enumerate(pieces):
        tokens = full // len(parts)
        for r, (rows, first) in enumerate(parts):
            at = (lax.broadcasted_iota(jnp.int32, (tokens, 128), 0) + first).astype(F32)
            for u in range(share):
                start = (s * share + u) * full + r * tokens
                place = slice(start, start + tokens)
                history_ref[place, :] = rows[u * tokens : (u + 1) * tokens]
                mask_ref[place, :] = jnp.where(at < turn[s][u : u + 1, :128], 0.0, -jnp.inf)
    key_ref[...] = jnp.dot(history_ref[...], w_key_ref[...], preferred_element_type=F32).astype(BF16)
    values = jnp.dot(history_ref[...], w_value_ref[...], preferred_element_type=F32).astype(BF16)
    pooled = jnp.dot(values, w_pooled_ref[...], preferred_element_type=F32)
    lane = lax.broadcasted_iota(jnp.int32, (hid, both), 1)
    one = lax.broadcasted_iota(jnp.int32, (2 * hid, hid), 0) % hid
    one = jnp.where(one == lax.broadcasted_iota(jnp.int32, (2 * hid, hid), 1), 1.0, 0.0).astype(BF16)
    for pair in range(pairs):
        flat = pooled[pair * both : (pair + 1) * both].T
        pooled_ref[pair, :hid, :both] = jnp.where(lane < full, flat, 0.0).astype(BF16)
        pooled_ref[pair, hid:, :both] = jnp.where(lane < full, 0.0, flat).astype(BF16)
        pooled_ref[pair, :, both:] = one


def score(items_ref, state, heads_ref, bias_ref, out_ref, scratch, shares):
    key_ref, pooled_ref, mask_ref = state
    scores_ref, weights_ref, hidden_ref = scratch
    width = key_ref.shape[1]
    tasks = heads_ref.shape[0] // 2
    pairs, hid, depth = pooled_ref.shape
    both = depth - hid // 2
    full = both // 2
    share = pairs // shares
    columns = items_ref.shape[1]
    factor = math.log2(math.e) / math.sqrt(width)

    scores_ref[...] = jnp.dot(key_ref[...], items_ref[:width, :], preferred_element_type=F32)
    for user in range(2 * pairs):
        rows = slice(user * full, (user + 1) * full)
        for column in range(0, columns, 128):
            lanes = slice(column, column + 128)
            scores = scores_ref[rows, lanes] + mask_ref[rows, :]
            maximum = jnp.max(scores, axis=0, keepdims=True)
            expo = jnp.exp2((scores - maximum) * factor)
            weights = expo * (1.0 / jnp.sum(expo, axis=0, keepdims=True))
            weights_ref[rows, lanes] = weights.astype(BF16)
    for pair in range(pairs):
        rows = slice(pair * both, (pair + 1) * both)
        inputs = jnp.concatenate([weights_ref[rows, :], items_ref[width:, :]], 0)
        hidden = jnp.dot(pooled_ref[pair], inputs, preferred_element_type=F32)
        hidden_ref[pair] = jnp.maximum(hidden, 0.0).astype(BF16)
    bias = jnp.concatenate([bias_ref[...]] * (columns // 128), 1)
    for pair in range(pairs):
        logits = jnp.dot(heads_ref[...], hidden_ref[pair], preferred_element_type=F32) + bias
        first = lax.rem(lax.axis_index("sub") + pair // share, shares) * share + pair % share
        if len(out_ref.shape) == 3:
            out_ref[2 * first] = logits[:tasks]
            out_ref[2 * first + 1] = logits[tasks:]
        else:
            place = pl.multiple_of(2 * first * tasks, 2 * tasks)
            out_ref[pl.ds(place, 2 * tasks), :] = logits.astype(out_ref.dtype)


def first_kernel(own, shares, parts, *refs):
    if own:
        history_ref, refs = refs[0], refs[1:]
    given = [own and s > 0 and r == 0 and parts > 1 for s in range(shares) for r in range(parts)]
    count = given.count(False)
    sent, refs = list(refs[:count]), refs[count:]
    piece_refs = [None if local else sent.pop(0) for local in given]
    w_key_ref, w_value_ref, w_pooled_ref, items_ref, heads_ref, bias_ref = refs[:6]
    out_ref, key_ref, pooled_ref, mask_ref, rows_ref, *scratch = refs[6:]
    me, side = lax.axis_index("users"), lax.axis_index("sub")
    pieces, turn = [], []
    rows = piece_refs[0].shape[0] - LENGTH_ROWS
    tokens = (pooled_ref.shape[2] - pooled_ref.shape[1] // 2) // 2 // parts
    for s in range(shares):
        entries = []
        for r in range(parts):
            ref = piece_refs[s * parts + r]
            if own and s > 0 and r == 0:
                users = history_ref.shape[0] // shares
                chosen = history_ref[pl.ds(lax.rem(side + s, shares) * users, users)]
                content = chosen.reshape(rows, history_ref.shape[2])
            else:
                content = ref[:rows, :]
            entries.append((content, lax.rem(me + r, parts) * tokens))
        pieces.append(entries)
        turn.append(piece_refs[s * parts + parts - 1][rows:, :].astype(F32))
    state = (key_ref, pooled_ref, mask_ref)
    keys_values(pieces, turn, w_key_ref, w_value_ref, w_pooled_ref, *state, rows_ref)
    score(items_ref, state, heads_ref, bias_ref, out_ref, scratch, shares)


def next_kernel(shares, items_ref, key_ref, pooled_ref, mask_ref, heads_ref, bias_ref, out_ref, *scratch):
    state = (key_ref, pooled_ref, mask_ref)
    score(items_ref, state, heads_ref, bias_ref, out_ref, scratch, shares)


def place_kernel(count, *refs):
    own_refs, away_refs, (out_ref, held, sems) = refs[:2], refs[2:count], refs[count:]
    users, _, tasks, _ = out_ref.shape
    me = lax.axis_index("blk")
    copies = []
    for at, ref in enumerate(own_refs):
        held[at] = ref[...]
    for at, ref in enumerate(away_refs):
        for user in range(0, users, 2):
            both = ref[user * tasks : (user + 2) * tasks, :].astype(F32)
            held[at + 2, user] = both[:tasks]
            held[at + 2, user + 1] = both[tasks:]
    for position in range(WIN):
        block = lax.rem(me + (position - REACH) % count, count)
        ahead = lax.rem(block // 2 - me // 2 + count // 2, count // 2)
        source = 2 * ahead + lax.rem(block + me, 2)
        copy = pltpu.make_async_copy(held.at[source], out_ref.at[:, position], sems.at[position])
        copy.start()
        copies.append(copy)
    for copy in copies:
        copy.wait()


def shift(block, axis, distance):
    count = lax.axis_size(axis)
    return lax.ppermute(block, axis, [((i + distance) % count, i) for i in range(count)])


def from_pair(block, distance):
    count = lax.axis_size("blk")
    return lax.ppermute(block, "blk", [((i + 2 * distance) % count, i) for i in range(count)])


def spread(piece, shares, parts, own=False):
    row = [piece]
    for r in range(1, parts):
        row.append(shift(piece, "users", r))
    table = [row]
    for s in range(1, shares):
        line = [None]
        for r in range(parts):
            if r or not own or parts == 1:
                entry = shift(row[r], "sub", s)
                line[r:] = [entry]
        table.append(line)
    return table


def shards(
    history,
    lengths,
    item_rows,
    w_query,
    w_item,
    w_key,
    w_value,
    w_pooled,
    w_joint,
    bias_hidden,
    w_task,
    bias_task,
):
    users, tokens, width = history.shape
    items = item_rows.shape[0]
    hid, tasks = w_task.shape
    count, parts, shares = (lax.axis_size(axis) for axis in ("blk", "users", "sub"))
    full = tokens * parts

    sources = (item_rows, w_query, w_item, w_joint, bias_hidden[None], w_task.T)
    piece, mine, heads, bias = call(
        functools.partial(prepare_kernel, shares),
        (
            pltpu.VMEM((users // shares * tokens + LENGTH_ROWS, width), BF16),
            pltpu.VMEM((width + hid, items), BF16),
            pltpu.VMEM((2 * tasks, 2 * hid), BF16),
            pltpu.VMEM((2 * tasks, 128), F32),
        ),
        [HBM] * 9,
        [VMEM] * 4,
        (history, *sources, bias_task, lengths),
        2 * items * item_rows.shape[1] * 2 * width,
        (
            *(pltpu.VMEM(a.shape, a.dtype) for a in sources),
            pltpu.SMEM(bias_task.shape, F32),
            pltpu.SMEM(lengths.shape, jnp.int32),
            pltpu.SemaphoreType.DMA((8,)),
            pltpu.SemaphoreType.DMA((users // shares,)),
        ),
    )
    flops = 2 * users * items * (full * (width + hid) + hid * tasks)
    state = (
        pltpu.VMEM((users * full, width), BF16),
        pltpu.VMEM((users // 2, 2 * hid, 2 * full + hid), BF16),
        pltpu.VMEM((users * full, 128), F32),
    )
    kept = pltpu.VMEM((users, tasks, items), F32)
    sent = pltpu.VMEM((users * tasks, items), BF16)
    scratch = (
        pltpu.VMEM((users * full, items), F32),
        pltpu.VMEM((users * full, items), BF16),
        pltpu.VMEM((users // 2, 2 * hid, items), BF16),
    )

    def start(table, block, out, own):
        flat = [entry for row in table for entry in row if entry is not None]
        head = [history] if own else []
        result = call(
            functools.partial(first_kernel, own, shares, parts),
            (out, *state),
            [VMEM] * (len(head) + len(flat) + 6),
            [VMEM] * 4,
            (*head, *flat, w_key, w_value, w_pooled, block, heads, bias),
            flops + 4 * users * full * width * width,
            (pltpu.VMEM((users * full, width), BF16), *scratch),
        )
        return result[0], result[1:]

    def go_on(held, block, out):
        return call(
            functools.partial(next_kernel, shares),
            out,
            [VMEM] * 6,
            VMEM,
            (block, *held, heads, bias),
            flops,
            scratch,
        )

    if count % 2 or count > WIN:
        window = [None] * WIN
        table = spread(piece, shares, parts, True)
        window[REACH], held = start(table, mine, kept, True)
        low = high = mine
        for offset in range(1, REACH + 1):
            low, high = shift(low, "blk", -1), shift(high, "blk", 1)
            window[REACH - offset] = go_on(held, low, kept)
            window[REACH + offset] = go_on(held, high, kept)
        return jnp.stack(window, axis=1)

    far = []
    for ahead in range(1, count // 2):
        far.append(from_pair(piece, ahead))
    other = lax.ppermute(mine, "blk", [(i ^ 1, i) for i in range(count)])
    own = spread(piece, shares, parts, True)
    at_home, held = start(own, mine, kept, True)
    away = []
    for ahead, entry in enumerate(far, 1):
        table = spread(entry, shares, parts)
        result, guests = start(table, mine, sent, False)
        back = [from_pair(result, -ahead)]
        result = go_on(guests, other, sent)
        back.append(from_pair(result, -ahead))
        away.append(back)
    beside = go_on(held, other, kept)
    results = [entry for back in reversed(away) for entry in back]
    return call(
        functools.partial(place_kernel, count),
        jax.ShapeDtypeStruct((users, WIN, tasks, items), F32),
        [VMEM] * count,
        HBM,
        (at_home, beside, *results),
        0,
        (pltpu.VMEM((count, users, tasks, items), F32), pltpu.SemaphoreType.DMA((WIN,))),
    )


def solution(mesh):
    placed = (
        P(("parts", "blk"), "users", None),
        P(("parts", "blk")),
        P(("parts", "blk", "users", "sub"), None),
        P(),
        P(),
        P(),
        P(),
        P(),
        P(),
        P(),
        P(),
        P(),
    )

    return jax.shard_map(
        shards,
        mesh=mesh,
        in_specs=placed,
        out_specs=P(("parts", "blk"), None, None, ("users", "sub")),
        check_vma=False,
    )
```

```python
import functools
import math

import jax
import jax.numpy as jnp
from jax import lax
from jax.experimental import pallas as pl
from jax.experimental.pallas import tpu as pltpu
from jax.sharding import PartitionSpec as P


REACH = 4
WIN = 2 * REACH + 1
LENGTH_ROWS = 16
KERNEL_BYTES = 16 << 20
BF16 = jnp.bfloat16
F32 = jnp.float32
VMEM = pl.BlockSpec(memory_space=pltpu.VMEM)
SMEM = pl.BlockSpec(memory_space=pltpu.SMEM)
HBM = pl.BlockSpec(memory_space=pltpu.HBM)


def call(kernel, out_shape, in_specs, out_specs, args, flops, scratch=()):
    moved = sum(math.prod(a.shape) * a.dtype.itemsize for a in args)
    spaces = {id(VMEM): pltpu.VMEM, id(HBM): pltpu.HBM}
    args = [pltpu.with_memory_space_constraint(a, spaces[id(spec)]) for a, spec in zip(args, in_specs)]
    return pl.pallas_call(
        kernel,
        out_shape=out_shape,
        in_specs=in_specs,
        out_specs=out_specs,
        scratch_shapes=list(scratch),
        compiler_params=pltpu.CompilerParams(vmem_limit_bytes=KERNEL_BYTES),
        cost_estimate=pl.CostEstimate(flops=flops, bytes_accessed=moved, transcendentals=0),
    )(*args)


def fetch_kernel(shares, *refs):
    history_ref, sources = refs[0], refs[1:9]
    piece_ref, heads_ref, bias_out, *fetched = refs[9:17]
    w_task_ref, bias_ref, lengths_ref, sems = refs[17:]
    users, tokens, _ = history_ref.shape
    users //= shares
    width = piece_ref.shape[1]
    first = lax.axis_index("sub") * users
    pairs = []
    for user in range(users):
        place = piece_ref.at[pl.ds(user * tokens, tokens)]
        pairs.append((history_ref.at[first + user], place))
    pairs += zip(sources, (lengths_ref, w_task_ref, bias_ref, *fetched))
    copies = [pltpu.make_async_copy(*pair, sems.at[i]) for i, pair in enumerate(pairs)]
    for copy in copies:
        copy.start()
    copies[users].wait()
    row = lax.broadcasted_iota(jnp.int32, (LENGTH_ROWS, width), 0)
    lengths = jnp.zeros((LENGTH_ROWS, width), F32)
    for user in range(users):
        lengths = jnp.where(row == user, lengths_ref[first + user].astype(F32), lengths)
    piece_ref[users * tokens :, :] = lengths.astype(BF16)
    copies[users + 1].wait()
    tasks, hid = w_task_ref.shape
    w_task = w_task_ref[...].astype(F32)
    blank = jnp.zeros_like(w_task)
    heads_ref[:, :hid] = jnp.concatenate([w_task, blank], 0).astype(BF16)
    heads_ref[:, hid:] = jnp.concatenate([blank, w_task], 0).astype(BF16)
    copies[users + 2].wait()
    row = lax.broadcasted_iota(jnp.int32, bias_out.shape, 0) % tasks
    bias = jnp.zeros(bias_out.shape, F32)
    for task in range(tasks):
        bias = jnp.where(row == task, bias_ref[task], bias)
    bias_out[...] = bias
    for copy in copies[:users] + copies[users + 3 :]:
        copy.wait()


def project_kernel(items_ref, w_query_ref, w_item_ref, w_joint_ref, bias_ref, out_ref):
    width = w_query_ref.shape[1]
    rows = items_ref[...]
    queries = jnp.dot(rows, w_query_ref[...], preferred_element_type=F32)
    out_ref[:width, :] = queries.T.astype(BF16)
    joined = jnp.dot(rows, w_item_ref[...], preferred_element_type=F32).astype(BF16)
    terms = jnp.dot(joined, w_joint_ref[...], preferred_element_type=F32) + bias_ref[...]
    out_ref[width:, :] = terms.T.astype(BF16)


def keys_values(pieces, turn, w_key_ref, w_value_ref, w_pooled_ref, key_ref, pooled_ref, mask_ref, history_ref):
    pairs, hid, depth = pooled_ref.shape
    hid //= 2
    both = depth - hid
    full = both // 2
    users = 2 * pairs
    share = users // len(pieces)
    for s, parts in enumerate(pieces):
        tokens = full // len(parts)
        for r, (rows, first) in enumerate(parts):
            at = (lax.broadcasted_iota(jnp.int32, (tokens, 128), 0) + first).astype(F32)
            for u in range(share):
                start = (s * share + u) * full + r * tokens
                place = slice(start, start + tokens)
                history_ref[place, :] = rows[u * tokens : (u + 1) * tokens]
                mask_ref[place, :] = jnp.where(at < turn[s][u : u + 1, :128], 0.0, -jnp.inf)
    key_ref[...] = jnp.dot(history_ref[...], w_key_ref[...], preferred_element_type=F32).astype(BF16)
    values = jnp.dot(history_ref[...], w_value_ref[...], preferred_element_type=F32).astype(BF16)
    pooled = jnp.dot(values, w_pooled_ref[...], preferred_element_type=F32)
    lane = lax.broadcasted_iota(jnp.int32, (hid, both), 1)
    one = lax.broadcasted_iota(jnp.int32, (2 * hid, hid), 0) % hid
    one = jnp.where(one == lax.broadcasted_iota(jnp.int32, (2 * hid, hid), 1), 1.0, 0.0).astype(BF16)
    for pair in range(pairs):
        flat = pooled[pair * both : (pair + 1) * both].T
        pooled_ref[pair, :hid, :both] = jnp.where(lane < full, flat, 0.0).astype(BF16)
        pooled_ref[pair, hid:, :both] = jnp.where(lane < full, 0.0, flat).astype(BF16)
        pooled_ref[pair, :, both:] = one


def score(items_ref, state, heads_ref, bias_ref, out_ref, scratch, shares):
    key_ref, pooled_ref, mask_ref = state
    scores_ref, weights_ref, hidden_ref = scratch
    width = key_ref.shape[1]
    tasks = heads_ref.shape[0] // 2
    pairs, hid, depth = pooled_ref.shape
    both = depth - hid // 2
    full = both // 2
    share = pairs // shares
    columns = items_ref.shape[1]
    factor = math.log2(math.e) / math.sqrt(width)

    scores_ref[...] = jnp.dot(key_ref[...], items_ref[:width, :], preferred_element_type=F32)
    for user in range(2 * pairs):
        rows = slice(user * full, (user + 1) * full)
        for column in range(0, columns, 128):
            lanes = slice(column, column + 128)
            scores = scores_ref[rows, lanes] + mask_ref[rows, :]
            maximum = jnp.max(scores, axis=0, keepdims=True)
            expo = jnp.exp2((scores - maximum) * factor)
            weights = expo * (1.0 / jnp.sum(expo, axis=0, keepdims=True))
            weights_ref[rows, lanes] = weights.astype(BF16)
    for pair in range(pairs):
        rows = slice(pair * both, (pair + 1) * both)
        inputs = jnp.concatenate([weights_ref[rows, :], items_ref[width:, :]], 0)
        hidden = jnp.dot(pooled_ref[pair], inputs, preferred_element_type=F32)
        hidden_ref[pair] = jnp.maximum(hidden, 0.0).astype(BF16)
    bias = jnp.concatenate([bias_ref[...]] * (columns // 128), 1)
    for pair in range(pairs):
        logits = jnp.dot(heads_ref[...], hidden_ref[pair], preferred_element_type=F32) + bias
        first = lax.rem(lax.axis_index("sub") + pair // share, shares) * share + pair % share
        if len(out_ref.shape) == 3:
            out_ref[2 * first] = logits[:tasks]
            out_ref[2 * first + 1] = logits[tasks:]
        else:
            place = pl.multiple_of(2 * first * tasks, 2 * tasks)
            out_ref[pl.ds(place, 2 * tasks), :] = logits.astype(out_ref.dtype)


def first_kernel(own, shares, parts, *refs):
    if own:
        history_ref, refs = refs[0], refs[1:]
    given = [own and s > 0 and r == 0 and parts > 1 for s in range(shares) for r in range(parts)]
    count = given.count(False)
    sent, refs = list(refs[:count]), refs[count:]
    piece_refs = [None if local else sent.pop(0) for local in given]
    w_key_ref, w_value_ref, w_pooled_ref, items_ref, heads_ref, bias_ref = refs[:6]
    out_ref, key_ref, pooled_ref, mask_ref, rows_ref, *scratch = refs[6:]
    me, side = lax.axis_index("users"), lax.axis_index("sub")
    pieces, turn = [], []
    rows = piece_refs[0].shape[0] - LENGTH_ROWS
    tokens = (pooled_ref.shape[2] - pooled_ref.shape[1] // 2) // 2 // parts
    for s in range(shares):
        entries = []
        for r in range(parts):
            ref = piece_refs[s * parts + r]
            if own and s > 0 and r == 0:
                users = history_ref.shape[0] // shares
                chosen = history_ref[pl.ds(lax.rem(side + s, shares) * users, users)]
                content = chosen.reshape(rows, history_ref.shape[2])
            else:
                content = ref[:rows, :]
            entries.append((content, lax.rem(me + r, parts) * tokens))
        pieces.append(entries)
        turn.append(piece_refs[s * parts + parts - 1][rows:, :].astype(F32))
    state = (key_ref, pooled_ref, mask_ref)
    keys_values(pieces, turn, w_key_ref, w_value_ref, w_pooled_ref, *state, rows_ref)
    score(items_ref, state, heads_ref, bias_ref, out_ref, scratch, shares)


def next_kernel(shares, items_ref, key_ref, pooled_ref, mask_ref, heads_ref, bias_ref, out_ref, *scratch):
    state = (key_ref, pooled_ref, mask_ref)
    score(items_ref, state, heads_ref, bias_ref, out_ref, scratch, shares)


def place_kernel(count, *refs):
    own_refs, away_refs, (out_ref, held, sems) = refs[:2], refs[2:count], refs[count:]
    users, _, tasks, _ = out_ref.shape
    me = lax.axis_index("blk")
    copies = []
    for at, ref in enumerate(own_refs):
        held[at] = ref[...]
    for at, ref in enumerate(away_refs):
        for user in range(0, users, 2):
            both = ref[user * tasks : (user + 2) * tasks, :].astype(F32)
            held[at + 2, user] = both[:tasks]
            held[at + 2, user + 1] = both[tasks:]
    for position in range(WIN):
        block = lax.rem(me + (position - REACH) % count, count)
        ahead = lax.rem(block // 2 - me // 2 + count // 2, count // 2)
        source = 2 * ahead + lax.rem(block + me, 2)
        copy = pltpu.make_async_copy(held.at[source], out_ref.at[:, position], sems.at[position])
        copy.start()
        copies.append(copy)
    for copy in copies:
        copy.wait()


def shift(block, axis, distance):
    count = lax.axis_size(axis)
    return lax.ppermute(block, axis, [((i + distance) % count, i) for i in range(count)])


def from_pair(block, distance):
    count = lax.axis_size("blk")
    return lax.ppermute(block, "blk", [((i + 2 * distance) % count, i) for i in range(count)])


def spread(piece, shares, parts, own=False):
    row = [piece]
    for r in range(1, parts):
        row.append(shift(piece, "users", r))
    table = [row]
    for s in range(1, shares):
        line = [None]
        for r in range(parts):
            if r or not own or parts == 1:
                entry = shift(row[r], "sub", s)
                line[r:] = [entry]
        table.append(line)
    return table


def shards(
    history,
    lengths,
    item_rows,
    w_query,
    w_item,
    w_key,
    w_value,
    w_pooled,
    w_joint,
    bias_hidden,
    w_task,
    bias_task,
):
    users, tokens, width = history.shape
    items = item_rows.shape[0]
    hid, tasks = w_task.shape
    count, parts, shares = (lax.axis_size(axis) for axis in ("blk", "users", "sub"))
    full = tokens * parts

    share = users // shares
    operands = (item_rows, w_query, w_item, w_joint, bias_hidden[None])
    piece, heads, bias, *fetched = call(
        functools.partial(fetch_kernel, shares),
        (
            pltpu.VMEM((share * tokens + LENGTH_ROWS, width), BF16),
            pltpu.VMEM((2 * tasks, 2 * hid), BF16),
            pltpu.VMEM((2 * tasks, 128), F32),
            *(pltpu.VMEM(a.shape, a.dtype) for a in operands),
        ),
        [HBM] * 9,
        [VMEM] * 8,
        (history, lengths, w_task.T, bias_task, *operands),
        0,
        (
            pltpu.VMEM((tasks, hid), BF16),
            pltpu.SMEM(bias_task.shape, F32),
            pltpu.SMEM(lengths.shape, jnp.int32),
            pltpu.SemaphoreType.DMA((share + 8,)),
        ),
    )
    mine = call(
        project_kernel,
        pltpu.VMEM((width + hid, items), BF16),
        [VMEM] * 5,
        VMEM,
        fetched,
        2 * items * item_rows.shape[1] * 2 * width,
    )
    flops = 2 * users * items * (full * (width + hid) + hid * tasks)
    state = (
        pltpu.VMEM((users * full, width), BF16),
        pltpu.VMEM((users // 2, 2 * hid, 2 * full + hid), BF16),
        pltpu.VMEM((users * full, 128), F32),
    )
    kept = pltpu.VMEM((users, tasks, items), F32)
    sent = pltpu.VMEM((users * tasks, items), BF16)
    scratch = (
        pltpu.VMEM((users * full, items), F32),
        pltpu.VMEM((users * full, items), BF16),
        pltpu.VMEM((users // 2, 2 * hid, items), BF16),
    )

    def start(table, block, out, own):
        flat = [entry for row in table for entry in row if entry is not None]
        head = [history] if own else []
        result = call(
            functools.partial(first_kernel, own, shares, parts),
            (out, *state),
            [VMEM] * (len(head) + len(flat) + 6),
            [VMEM] * 4,
            (*head, *flat, w_key, w_value, w_pooled, block, heads, bias),
            flops + 4 * users * full * width * width,
            (pltpu.VMEM((users * full, width), BF16), *scratch),
        )
        return result[0], result[1:]

    def go_on(held, block, out):
        return call(
            functools.partial(next_kernel, shares),
            out,
            [VMEM] * 6,
            VMEM,
            (block, *held, heads, bias),
            flops,
            scratch,
        )

    if count % 2 or count > WIN:
        window = [None] * WIN
        table = spread(piece, shares, parts, True)
        window[REACH], held = start(table, mine, kept, True)
        low = high = mine
        for offset in range(1, REACH + 1):
            low, high = shift(low, "blk", -1), shift(high, "blk", 1)
            window[REACH - offset] = go_on(held, low, kept)
            window[REACH + offset] = go_on(held, high, kept)
        return jnp.stack(window, axis=1)

    far = []
    for ahead in range(1, count // 2):
        far.append(from_pair(piece, ahead))
    other = lax.ppermute(mine, "blk", [(i ^ 1, i) for i in range(count)])
    own = spread(piece, shares, parts, True)
    at_home, held = start(own, mine, kept, True)
    away = []
    for ahead, entry in enumerate(far, 1):
        table = spread(entry, shares, parts)
        result, guests = start(table, mine, sent, False)
        back = [from_pair(result, -ahead)]
        result = go_on(guests, other, sent)
        back.append(from_pair(result, -ahead))
        away.append(back)
    beside = go_on(held, other, kept)
    results = [entry for back in reversed(away) for entry in back]
    return call(
        functools.partial(place_kernel, count),
        jax.ShapeDtypeStruct((users, WIN, tasks, items), F32),
        [VMEM] * count,
        HBM,
        (at_home, beside, *results),
        0,
        (pltpu.VMEM((count, users, tasks, items), F32), pltpu.SemaphoreType.DMA((WIN,))),
    )


def solution(mesh):
    placed = (
        P(("parts", "blk"), "users", None),
        P(("parts", "blk")),
        P(("parts", "blk", "users", "sub"), None),
        P(),
        P(),
        P(),
        P(),
        P(),
        P(),
        P(),
        P(),
        P(),
    )

    return jax.shard_map(
        shards,
        mesh=mesh,
        in_specs=placed,
        out_specs=P(("parts", "blk"), None, None, ("users", "sub")),
        check_vma=False,
    )
```

```python
import functools
import math

import jax
import jax.numpy as jnp
from jax import lax
from jax.experimental import pallas as pl
from jax.experimental.pallas import tpu as pltpu
from jax.sharding import PartitionSpec as P


REACH = 4
WIN = 2 * REACH + 1
LENGTH_ROWS = 8
KERNEL_BYTES = 16 << 20
BF16 = jnp.bfloat16
F32 = jnp.float32
VMEM = pl.BlockSpec(memory_space=pltpu.VMEM)
SMEM = pl.BlockSpec(memory_space=pltpu.SMEM)
HBM = pl.BlockSpec(memory_space=pltpu.HBM)


def call(kernel, out_shape, in_specs, out_specs, args, flops, scratch=(), aliases=None):
    moved = sum(math.prod(a.shape) * a.dtype.itemsize for a in args)
    spaces = {id(VMEM): pltpu.VMEM, id(HBM): pltpu.HBM}
    args = [pltpu.with_memory_space_constraint(a, spaces[id(spec)]) for a, spec in zip(args, in_specs)]
    return pl.pallas_call(
        kernel,
        out_shape=out_shape,
        in_specs=in_specs,
        out_specs=out_specs,
        scratch_shapes=list(scratch),
        input_output_aliases=aliases or {},
        compiler_params=pltpu.CompilerParams(vmem_limit_bytes=KERNEL_BYTES),
        cost_estimate=pl.CostEstimate(flops=flops, bytes_accessed=moved, transcendentals=0),
    )(*args)


def pack_kernel(shares, history_ref, lengths_ref, piece_ref, held_ref, sems):
    users, tokens, _ = history_ref.shape
    users //= shares
    width = piece_ref.shape[1]
    first = lax.axis_index("sub") * users
    copies = [pltpu.make_async_copy(lengths_ref, held_ref, sems.at[users])]
    for user in range(users):
        place = piece_ref.at[pl.ds(user * tokens, tokens)]
        copies.append(pltpu.make_async_copy(history_ref.at[first + user], place, sems.at[user]))
    for copy in copies:
        copy.start()
    copies[0].wait()
    row = lax.broadcasted_iota(jnp.int32, (LENGTH_ROWS, width), 0)
    lengths = jnp.zeros((LENGTH_ROWS, width), F32)
    for user in range(users):
        lengths = jnp.where(row == user, held_ref[first + user].astype(F32), lengths)
    piece_ref[users * tokens :, :] = lengths.astype(BF16)
    for copy in copies[1:]:
        copy.wait()


def project_kernel(*refs):
    sources, (out_ref, heads_ref, bias_out), held, sems = refs[:7], refs[7:10], refs[10:17], refs[17]
    copies = [pltpu.make_async_copy(*pair, sems.at[i]) for i, pair in enumerate(zip(sources, held))]
    for copy in copies:
        copy.start()
    items_ref, w_query_ref, w_item_ref, w_joint_ref, bias_ref, w_task_ref, bias_task_ref = held
    for copy in copies[5:]:
        copy.wait()
    tasks, hid = w_task_ref.shape
    w_task = w_task_ref[...].astype(F32)
    blank = jnp.zeros_like(w_task)
    heads_ref[:, :hid] = jnp.concatenate([w_task, blank], 0).astype(BF16)
    heads_ref[:, hid:] = jnp.concatenate([blank, w_task], 0).astype(BF16)
    row = lax.broadcasted_iota(jnp.int32, bias_out.shape, 0) % tasks
    bias = jnp.zeros(bias_out.shape, F32)
    for task in range(tasks):
        bias = jnp.where(row == task, bias_task_ref[task], bias)
    bias_out[...] = bias
    for copy in copies[:5]:
        copy.wait()
    width = w_query_ref.shape[1]
    rows = items_ref[...]
    queries = jnp.dot(rows, w_query_ref[...], preferred_element_type=F32)
    out_ref[:width, :] = queries.T.astype(BF16)
    joined = jnp.dot(rows, w_item_ref[...], preferred_element_type=F32).astype(BF16)
    terms = jnp.dot(joined, w_joint_ref[...], preferred_element_type=F32) + bias_ref[...]
    out_ref[width:, :] = terms.T.astype(BF16)


def keys_values(pieces, turn, w_key_ref, w_value_ref, w_pooled_ref, key_ref, pooled_ref, mask_ref, history_ref):
    pairs, hid, depth = pooled_ref.shape
    hid //= 2
    both = depth - hid
    full = both // 2
    users = 2 * pairs
    share = users // len(pieces)
    for s, parts in enumerate(pieces):
        tokens = full // len(parts)
        for r, (rows, first) in enumerate(parts):
            at = (lax.broadcasted_iota(jnp.int32, (tokens, 128), 0) + first).astype(F32)
            for u in range(share):
                start = (s * share + u) * full + r * tokens
                place = slice(start, start + tokens)
                history_ref[place, :] = rows[u * tokens : (u + 1) * tokens]
                mask_ref[place, :] = jnp.where(at < turn[s][u : u + 1, :128], 0.0, -jnp.inf)
    key_ref[...] = jnp.dot(history_ref[...], w_key_ref[...], preferred_element_type=F32).astype(BF16)
    values = jnp.dot(history_ref[...], w_value_ref[...], preferred_element_type=F32).astype(BF16)
    pooled = jnp.dot(values, w_pooled_ref[...], preferred_element_type=F32)
    lane = lax.broadcasted_iota(jnp.int32, (hid, both), 1)
    one = lax.broadcasted_iota(jnp.int32, (2 * hid, hid), 0) % hid
    one = jnp.where(one == lax.broadcasted_iota(jnp.int32, (2 * hid, hid), 1), 1.0, 0.0).astype(BF16)
    for pair in range(pairs):
        flat = pooled[pair * both : (pair + 1) * both].T
        pooled_ref[pair, :hid, :both] = jnp.where(lane < full, flat, 0.0).astype(BF16)
        pooled_ref[pair, hid:, :both] = jnp.where(lane < full, 0.0, flat).astype(BF16)
        pooled_ref[pair, :, both:] = one


def score(items_ref, state, heads_ref, bias_ref, out_ref, scratch, shares):
    key_ref, pooled_ref, mask_ref = state
    scores_ref, weights_ref, hidden_ref = scratch
    width = key_ref.shape[1]
    tasks = heads_ref.shape[0] // 2
    pairs, hid, depth = pooled_ref.shape
    both = depth - hid // 2
    full = both // 2
    share = pairs // shares
    columns = items_ref.shape[1]
    factor = math.log2(math.e) / math.sqrt(width)

    scores_ref[...] = jnp.dot(key_ref[...], items_ref[:width, :], preferred_element_type=F32)
    for user in range(2 * pairs):
        rows = slice(user * full, (user + 1) * full)
        for column in range(0, columns, 128):
            lanes = slice(column, column + 128)
            scores = scores_ref[rows, lanes] + mask_ref[rows, :]
            maximum = jnp.max(scores, axis=0, keepdims=True)
            expo = jnp.exp2((scores - maximum) * factor)
            weights = expo * (1.0 / jnp.sum(expo, axis=0, keepdims=True))
            weights_ref[rows, lanes] = weights.astype(BF16)
    for pair in range(pairs):
        rows = slice(pair * both, (pair + 1) * both)
        inputs = jnp.concatenate([weights_ref[rows, :], items_ref[width:, :]], 0)
        hidden = jnp.dot(pooled_ref[pair], inputs, preferred_element_type=F32)
        hidden_ref[pair] = jnp.maximum(hidden, 0.0).astype(BF16)
    bias = jnp.concatenate([bias_ref[...]] * (columns // 128), 1)
    for pair in range(pairs):
        logits = jnp.dot(heads_ref[...], hidden_ref[pair], preferred_element_type=F32) + bias
        first = lax.rem(lax.axis_index("sub") + pair // share, shares) * share + pair % share
        if len(out_ref.shape) == 3:
            out_ref[2 * first] = logits[:tasks]
            out_ref[2 * first + 1] = logits[tasks:]
        else:
            place = pl.multiple_of(2 * first * tasks, 2 * tasks)
            out_ref[pl.ds(place, 2 * tasks), :] = logits.astype(out_ref.dtype)


def first_kernel(own, shares, parts, *refs):
    if own:
        history_ref, refs = refs[0], refs[1:]
    given = [own and s > 0 and r == 0 and parts > 1 for s in range(shares) for r in range(parts)]
    count = given.count(False)
    sent, refs = list(refs[:count]), refs[count:]
    piece_refs = [None if local else sent.pop(0) for local in given]
    w_key_ref, w_value_ref, w_pooled_ref, items_ref, heads_ref, bias_ref = refs[:6]
    out_ref, key_ref, pooled_ref, mask_ref, rows_ref, *scratch = refs[6:]
    me, side = lax.axis_index("users"), lax.axis_index("sub")
    pieces, turn = [], []
    rows = piece_refs[0].shape[0] - LENGTH_ROWS
    tokens = (pooled_ref.shape[2] - pooled_ref.shape[1] // 2) // 2 // parts
    for s in range(shares):
        entries = []
        for r in range(parts):
            ref = piece_refs[s * parts + r]
            if own and s > 0 and r == 0:
                users = history_ref.shape[0] // shares
                chosen = history_ref[pl.ds(lax.rem(side + s, shares) * users, users)]
                content = chosen.reshape(rows, history_ref.shape[2])
            else:
                content = ref[:rows, :]
            entries.append((content, lax.rem(me + r, parts) * tokens))
        pieces.append(entries)
        turn.append(piece_refs[s * parts + parts - 1][rows:, :].astype(F32))
    state = (key_ref, pooled_ref, mask_ref)
    keys_values(pieces, turn, w_key_ref, w_value_ref, w_pooled_ref, *state, rows_ref)
    score(items_ref, state, heads_ref, bias_ref, out_ref, scratch, shares)


def next_kernel(shares, items_ref, key_ref, pooled_ref, mask_ref, heads_ref, bias_ref, out_ref, *scratch):
    state = (key_ref, pooled_ref, mask_ref)
    score(items_ref, state, heads_ref, bias_ref, out_ref, scratch, shares)


def place_own_kernel(home_ref, beside_ref, out_ref, sems):
    even = lax.rem(lax.axis_index("blk"), 2)
    places = [(home_ref, k) for k in range(0, WIN, REACH)]
    places += [(beside_ref, 1 + 2 * even), (beside_ref, 1 + 2 * even + REACH)]
    copies = [pltpu.make_async_copy(a, out_ref.at[:, k], sems.at[i]) for i, (a, k) in enumerate(places)]
    for copy in copies:
        copy.start()
    for copy in copies:
        copy.wait()


def place_away_kernel(*refs):
    *backs, _, out_ref, held, sems = refs
    _, users, tasks, _ = held.shape
    odd = 3 - 2 * lax.rem(lax.axis_index("blk"), 2)
    copies = []
    for at, (back_ref, first) in enumerate(zip(backs, (2, odd))):
        for user in range(0, users, 2):
            both = back_ref[user * tasks : (user + 2) * tasks, :].astype(F32)
            held[at, user] = both[:tasks]
            held[at, user + 1] = both[tasks:]
        for k in range(2):
            place = out_ref.at[:, first + k * REACH]
            copies.append(pltpu.make_async_copy(held.at[at], place, sems.at[2 * at + k]))
            copies[-1].start()
    for copy in copies:
        copy.wait()


def shift(block, axis, distance):
    count = lax.axis_size(axis)
    return lax.ppermute(block, axis, [((i + distance) % count, i) for i in range(count)])


def spread(piece, shares, parts, own=False):
    row = [piece]
    for r in range(1, parts):
        row.append(shift(piece, "users", r))
    table = [row]
    for s in range(1, shares):
        line = [None]
        for r in range(parts):
            if r or not own or parts == 1:
                entry = shift(row[r], "sub", s)
                line[r:] = [entry]
        table.append(line)
    return table


def shards(
    history,
    lengths,
    item_rows,
    w_query,
    w_item,
    w_key,
    w_value,
    w_pooled,
    w_joint,
    bias_hidden,
    w_task,
    bias_task,
):
    users, tokens, width = history.shape
    items = item_rows.shape[0]
    hid, tasks = w_task.shape
    count, parts, shares = (lax.axis_size(axis) for axis in ("blk", "users", "sub"))
    full = tokens * parts

    share = users // shares
    piece = call(
        functools.partial(pack_kernel, shares),
        pltpu.VMEM((share * tokens + LENGTH_ROWS, width), BF16),
        [HBM] * 2,
        VMEM,
        (history, lengths),
        0,
        (pltpu.SMEM(lengths.shape, jnp.int32), pltpu.SemaphoreType.DMA((share + 1,))),
    )
    operands = (item_rows, w_query, w_item, w_joint, bias_hidden[None], w_task.T)
    mine, heads, bias = call(
        project_kernel,
        (
            pltpu.VMEM((width + hid, items), BF16),
            pltpu.VMEM((2 * tasks, 2 * hid), BF16),
            pltpu.VMEM((2 * tasks, 128), F32),
        ),
        [HBM] * 7,
        [VMEM] * 3,
        (*operands, bias_task),
        2 * items * item_rows.shape[1] * 2 * width,
        (
            *(pltpu.VMEM(a.shape, a.dtype) for a in operands),
            pltpu.SMEM(bias_task.shape, F32),
            pltpu.SemaphoreType.DMA((7,)),
        ),
    )
    flops = 2 * users * items * (full * (width + hid) + hid * tasks)
    state = (
        pltpu.VMEM((users * full, width), BF16),
        pltpu.VMEM((users // 2, 2 * hid, 2 * full + hid), BF16),
        pltpu.VMEM((users * full, 128), F32),
    )
    kept = pltpu.VMEM((users, tasks, items), F32)
    sent = pltpu.VMEM((users * tasks, items), BF16)
    scratch = (
        pltpu.VMEM((users * full, items), F32),
        pltpu.VMEM((users * full, items), BF16),
        pltpu.VMEM((users // 2, 2 * hid, items), BF16),
    )

    def start(table, block, out, own):
        flat = [entry for row in table for entry in row if entry is not None]
        head = [history] if own else []
        result = call(
            functools.partial(first_kernel, own, shares, parts),
            (out, *state),
            [VMEM] * (len(head) + len(flat) + 6),
            [VMEM] * 4,
            (*head, *flat, w_key, w_value, w_pooled, block, heads, bias),
            flops + 4 * users * full * width * width,
            (pltpu.VMEM((users * full, width), BF16), *scratch),
        )
        return result[0], result[1:]

    def go_on(held, block, out):
        return call(
            functools.partial(next_kernel, shares),
            out,
            [VMEM] * 6,
            VMEM,
            (block, *held, heads, bias),
            flops,
            scratch,
        )

    if count != REACH:
        window = [None] * WIN
        table = spread(piece, shares, parts, True)
        window[REACH], held = start(table, mine, kept, True)
        low = high = mine
        for offset in range(1, REACH + 1):
            low, high = shift(low, "blk", -1), shift(high, "blk", 1)
            window[REACH - offset] = go_on(held, low, kept)
            window[REACH + offset] = go_on(held, high, kept)
        return jnp.stack(window, axis=1)

    across = [(i ^ 2, i) for i in range(count)]
    far = lax.ppermute(piece, "blk", across)
    other = lax.ppermute(mine, "blk", [(i ^ 1, i) for i in range(count)])
    table = spread(far, shares, parts)
    own = spread(piece, shares, parts, True)
    result, guests = start(table, mine, sent, False)
    first = lax.ppermute(result, "blk", across)
    result = go_on(guests, other, sent)
    second = lax.ppermute(result, "blk", across)
    at_home, held = start(own, mine, kept, True)
    beside = go_on(held, other, kept)
    whole = jax.ShapeDtypeStruct((users, WIN, tasks, items), F32)
    semaphores = pltpu.SemaphoreType.DMA((5,))
    out = call(place_own_kernel, whole, [VMEM] * 2, HBM, (at_home, beside), 0, (semaphores,))
    held = (pltpu.VMEM((2, users, tasks, items), F32), pltpu.SemaphoreType.DMA((4,)))
    specs = [VMEM, VMEM, HBM]
    return call(place_away_kernel, whole, specs, HBM, (first, second, out), 0, held, {2: 0})


def solution(mesh):
    placed = (
        P(("parts", "blk"), "users", None),
        P(("parts", "blk")),
        P(("parts", "blk", "users", "sub"), None),
        P(),
        P(),
        P(),
        P(),
        P(),
        P(),
        P(),
        P(),
        P(),
    )

    return jax.shard_map(
        shards,
        mesh=mesh,
        in_specs=placed,
        out_specs=P(("parts", "blk"), None, None, ("users", "sub")),
        check_vma=False,
    )
```

```python
import functools
import math

import jax
import jax.numpy as jnp
from jax import lax
from jax.experimental import pallas as pl
from jax.experimental.pallas import tpu as pltpu
from jax.sharding import PartitionSpec as P


REACH = 4
WIN = 2 * REACH + 1
LENGTH_ROWS = 8
KERNEL_BYTES = 16 << 20
BF16 = jnp.bfloat16
F32 = jnp.float32
VMEM = pl.BlockSpec(memory_space=pltpu.VMEM)
SMEM = pl.BlockSpec(memory_space=pltpu.SMEM)
HBM = pl.BlockSpec(memory_space=pltpu.HBM)


def call(kernel, out_shape, in_specs, out_specs, args, flops, scratch=(), aliases=None):
    moved = sum(math.prod(a.shape) * a.dtype.itemsize for a in args)
    spaces = {id(VMEM): pltpu.VMEM, id(HBM): pltpu.HBM}
    args = [pltpu.with_memory_space_constraint(a, spaces[id(spec)]) for a, spec in zip(args, in_specs)]
    return pl.pallas_call(
        kernel,
        out_shape=out_shape,
        in_specs=in_specs,
        out_specs=out_specs,
        scratch_shapes=list(scratch),
        input_output_aliases=aliases or {},
        compiler_params=pltpu.CompilerParams(vmem_limit_bytes=KERNEL_BYTES),
        cost_estimate=pl.CostEstimate(flops=flops, bytes_accessed=moved, transcendentals=0),
    )(*args)


def pack_kernel(shares, history_ref, lengths_ref, piece_ref, held_ref, sems):
    users, tokens, _ = history_ref.shape
    users //= shares
    width = piece_ref.shape[1]
    first = lax.axis_index("sub") * users
    copies = [pltpu.make_async_copy(lengths_ref, held_ref, sems.at[users])]
    for user in range(users):
        place = piece_ref.at[pl.ds(user * tokens, tokens)]
        copies.append(pltpu.make_async_copy(history_ref.at[first + user], place, sems.at[user]))
    for copy in copies:
        copy.start()
    copies[0].wait()
    row = lax.broadcasted_iota(jnp.int32, (LENGTH_ROWS, width), 0)
    lengths = jnp.zeros((LENGTH_ROWS, width), F32)
    for user in range(users):
        lengths = jnp.where(row == user, held_ref[first + user].astype(F32), lengths)
    piece_ref[users * tokens :, :] = lengths.astype(BF16)
    for copy in copies[1:]:
        copy.wait()


def project_kernel(*refs):
    sources, (out_ref, heads_ref, bias_out), held, sems = refs[:7], refs[7:10], refs[10:17], refs[17]
    copies = [pltpu.make_async_copy(*pair, sems.at[i]) for i, pair in enumerate(zip(sources, held))]
    for copy in copies:
        copy.start()
    items_ref, w_query_ref, w_item_ref, w_joint_ref, bias_ref, w_task_ref, bias_task_ref = held
    for copy in copies[5:]:
        copy.wait()
    tasks, hid = w_task_ref.shape
    w_task = w_task_ref[...].astype(F32)
    blank = jnp.zeros_like(w_task)
    heads_ref[:, :hid] = jnp.concatenate([w_task, blank], 0).astype(BF16)
    heads_ref[:, hid:] = jnp.concatenate([blank, w_task], 0).astype(BF16)
    row = lax.broadcasted_iota(jnp.int32, bias_out.shape, 0) % tasks
    bias = jnp.zeros(bias_out.shape, F32)
    for task in range(tasks):
        bias = jnp.where(row == task, bias_task_ref[task], bias)
    bias_out[...] = bias
    for copy in copies[:5]:
        copy.wait()
    width = w_query_ref.shape[1]
    rows = items_ref[...]
    queries = jnp.dot(rows, w_query_ref[...], preferred_element_type=F32)
    out_ref[:width, :] = queries.T.astype(BF16)
    joined = jnp.dot(rows, w_item_ref[...], preferred_element_type=F32).astype(BF16)
    terms = jnp.dot(joined, w_joint_ref[...], preferred_element_type=F32) + bias_ref[...]
    out_ref[width:, :] = terms.T.astype(BF16)


def project_tokens(rows_ref, weights):
    w_key_ref, w_value_ref, w_pooled_ref = weights
    keys = jnp.dot(rows_ref[...], w_key_ref[...], preferred_element_type=F32).astype(BF16)
    values = jnp.dot(rows_ref[...], w_value_ref[...], preferred_element_type=F32).astype(BF16)
    return keys, jnp.dot(values, w_pooled_ref[...], preferred_element_type=F32)


def arrange(pooled, firsts, lengths, state):
    _, pooled_ref, mask_ref = state
    pairs, hid, depth = pooled_ref.shape
    hid //= 2
    both = depth - hid
    full = both // 2
    parts = len(firsts)
    tokens = full // parts
    for r, first in enumerate(firsts):
        at = (lax.broadcasted_iota(jnp.int32, (tokens, 128), 0) + first).astype(F32)
        for user in range(2 * pairs):
            start = user * full + r * tokens
            valid = at < lengths[user : user + 1, :128]
            mask_ref[start : start + tokens, :] = jnp.where(valid, 0.0, -jnp.inf)
    lane = lax.broadcasted_iota(jnp.int32, (hid, both), 1)
    one = lax.broadcasted_iota(jnp.int32, (2 * hid, hid), 0) % hid
    one = jnp.where(one == lax.broadcasted_iota(jnp.int32, (2 * hid, hid), 1), 1.0, 0.0).astype(BF16)
    for pair in range(pairs):
        rows = [pooled(user, r) for user in (2 * pair, 2 * pair + 1) for r in range(parts)]
        flat = jnp.concatenate(rows, 0).T
        pooled_ref[pair, :hid, :both] = jnp.where(lane < full, flat, 0.0).astype(BF16)
        pooled_ref[pair, hid:, :both] = jnp.where(lane < full, 0.0, flat).astype(BF16)
        pooled_ref[pair, :, both:] = one


def score(items_ref, parts, states, heads_ref, bias_ref, scratch, put, late=None):
    scores_ref, weights_ref, hidden_ref = scratch
    width = states[0][0].shape[1]
    columns = items_ref.shape[1]
    factor = math.log2(math.e) / math.sqrt(width)
    bias = jnp.concatenate([bias_ref[...]] * (columns // 128), 1)
    count = states[0][0].shape[0]
    pairs, hid, depth = states[0][1].shape
    both = depth - hid // 2
    full = both // 2
    tokens = full // parts
    if late:
        early_ref, keys = late
    else:
        keys = jnp.concatenate([key_ref[...] for key_ref, _, _ in states], 0)
    scores = jnp.dot(keys, items_ref[:width, :], preferred_element_type=F32)
    scores_ref[: keys.shape[0], :] = scores
    for at, (_, _, mask_ref) in enumerate(states):
        for user in range(2 * pairs):
            rows = slice(user * full, (user + 1) * full)
            place = slice(at * count + user * full, at * count + (user + 1) * full)
            for column in range(0, columns, 128):
                lanes = slice(column, column + 128)
                if late:
                    found = [early_ref[user * tokens : (user + 1) * tokens, lanes]]
                    for r in range(parts - 1):
                        start = (r * 2 * pairs + user) * tokens
                        found.append(scores_ref[start : start + tokens, lanes])
                    scores = jnp.concatenate(found, 0)
                else:
                    scores = scores_ref[place, lanes]
                scores = scores + mask_ref[rows, :]
                maximum = jnp.max(scores, axis=0, keepdims=True)
                expo = jnp.exp2((scores - maximum) * factor)
                weights = expo * (1.0 / jnp.sum(expo, axis=0, keepdims=True))
                weights_ref[place, lanes] = weights.astype(BF16)
    turns = [(at, pair) for at in range(len(states)) for pair in range(pairs)]
    for at, pair in turns:
        start = at * count + pair * both
        inputs = jnp.concatenate([weights_ref[start : start + both, :], items_ref[width:, :]], 0)
        hidden = jnp.dot(states[at][1][pair], inputs, preferred_element_type=F32)
        hidden_ref[at * pairs + pair] = jnp.maximum(hidden, 0.0).astype(BF16)
    for at, pair in turns:
        hidden = hidden_ref[at * pairs + pair]
        put(at, pair, jnp.dot(heads_ref[...], hidden, preferred_element_type=F32) + bias)


def keep(out_ref, shares, pairs):
    tasks = out_ref.shape[1] if len(out_ref.shape) == 3 else None

    def put(share, pair, logits):
        user = 2 * (lax.rem(lax.axis_index("sub") + share, shares) * pairs + pair)
        count = logits.shape[0] // 2
        if tasks:
            out_ref[user] = logits[:count]
            out_ref[user + 1] = logits[count:]
        else:
            place = pl.multiple_of(user * count, 2 * count)
            out_ref[pl.ds(place, 2 * count), :] = logits.astype(out_ref.dtype)

    return put


def own_kernel(shares, parts, *refs):
    history_ref, *refs = refs
    given = shares * parts - (shares - 1 if parts > 1 else 0)
    pieces, refs = refs[:given], refs[given:]
    weights, (items_ref, heads_ref, bias_ref, out_ref), refs = refs[:3], refs[3:7], refs[7:]
    states = [tuple(refs[3 * s : 3 * s + 3]) for s in range(shares)]
    rows_ref, *scratch = refs[3 * shares :]
    side, me = lax.axis_index("sub"), lax.axis_index("users")
    users, tokens, width = history_ref.shape
    count = users // shares * tokens
    for s in range(shares):
        for r in range(parts):
            if s and not r and parts > 1:
                chosen = history_ref[pl.ds(lax.rem(side + s, shares) * (users // shares), users // shares)]
                rows = chosen.reshape(count, width)
            else:
                last = pieces.pop(0)
                rows = last[:count, :]
            for user in range(users // shares):
                start = (user * parts + r) * tokens
                rows_ref[s, start : start + tokens, :] = rows[user * tokens : (user + 1) * tokens]
        lengths = last[count:, :].astype(F32)
        keys, values = project_tokens(rows_ref.at[s], weights)
        states[s][0][...] = keys

        def pooled(user, r):
            start = (user * parts + r) * tokens
            return values[start : start + tokens]

        arrange(pooled, [lax.rem(me + r, parts) * tokens for r in range(parts)], lengths, states[s])
    put = keep(out_ref, shares, states[0][1].shape[0])
    score(items_ref, parts, states, heads_ref, bias_ref, scratch, put)


def early_kernel(*refs):
    *pieces, w_key_ref, w_value_ref, w_pooled_ref, items_ref = refs[:-4]
    key_ref, values_ref, scores_ref, rows_ref = refs[-4:]
    count = rows_ref.shape[0] // len(pieces)
    for s, ref in enumerate(pieces):
        rows_ref[s * count : (s + 1) * count, :] = ref[:count, :]
    keys, values = project_tokens(rows_ref, (w_key_ref, w_value_ref, w_pooled_ref))
    key_ref[...] = keys
    values_ref[...] = values
    queries = items_ref[: keys.shape[1], :]
    scores_ref[...] = jnp.dot(keys, queries, preferred_element_type=F32)


def share_kernel(shares, parts, share, *refs):
    late, early, weights, refs = refs[: parts - 1], refs[parts - 1 : parts + 2], refs[parts + 2 : parts + 5], refs[parts + 5 :]
    (items_ref, heads_ref, bias_ref), refs = refs[:3], refs[3:]
    before = share if share == shares - 1 else 0
    earlier, refs = refs[:before], refs[before:]
    out_ref, state, rows_ref, scratch = refs[0], tuple(refs[1:4]), refs[4], refs[5:]
    me, side = lax.axis_index("users"), lax.axis_index("sub")
    count = rows_ref.shape[0] // (parts - 1)
    pairs = state[1].shape[0]
    tokens = count // (2 * pairs)
    for r, ref in enumerate(late):
        rows_ref[r * count : (r + 1) * count, :] = ref[:count, :]
    lengths = late[-1][count:, :].astype(F32)
    keys, values = project_tokens(rows_ref, weights)
    held = slice(share * count, (share + 1) * count)
    for user in range(2 * pairs):
        start = user * parts * tokens
        first = share * count + user * tokens
        state[0][start : start + tokens, :] = early[0][first : first + tokens, :]
        for r in range(parts - 1):
            start += tokens
            first = (r * 2 * pairs + user) * tokens
            state[0][start : start + tokens, :] = keys[first : first + tokens]

    def pooled(user, r):
        if r == 0:
            start = share * count + user * tokens
            return early[1][start : start + tokens, :]
        start = ((r - 1) * 2 * pairs + user) * tokens
        return values[start : start + tokens]

    arrange(pooled, [lax.rem(me + r, parts) * tokens for r in range(parts)], lengths, state)
    if share == shares - 1:
        whole = keep(out_ref, shares, pairs)
        size = out_ref.shape[0] // shares
        for s, ref in enumerate(earlier):
            place = pl.multiple_of(lax.rem(side + s, shares) * size, size)
            out_ref[pl.ds(place, size), :] = ref[...]
        put = lambda _, pair, logits: whole(share, pair, logits)
    else:

        def put(_, pair, logits):
            size = logits.shape[0]
            out_ref[pair * size : (pair + 1) * size, :] = logits.astype(out_ref.dtype)

    score(items_ref, parts, (state,), heads_ref, bias_ref, scratch, put, (early[2].at[held, :], keys))


def next_kernel(shares, parts, items_ref, *refs):
    states = [tuple(refs[3 * s : 3 * s + 3]) for s in range(shares)]
    heads_ref, bias_ref, out_ref, *scratch = refs[3 * shares :]
    put = keep(out_ref, shares, states[0][1].shape[0])
    score(items_ref, parts, states, heads_ref, bias_ref, scratch, put)


def place_own_kernel(home_ref, beside_ref, out_ref, sems):
    even = lax.rem(lax.axis_index("blk"), 2)
    places = [(home_ref, k) for k in range(0, WIN, REACH)]
    places += [(beside_ref, 1 + 2 * even), (beside_ref, 1 + 2 * even + REACH)]
    copies = [pltpu.make_async_copy(a, out_ref.at[:, k], sems.at[i]) for i, (a, k) in enumerate(places)]
    for copy in copies:
        copy.start()
    for copy in copies:
        copy.wait()


def place_away_kernel(*refs):
    *backs, _, out_ref, held, sems = refs
    _, users, tasks, _ = held.shape
    odd = 3 - 2 * lax.rem(lax.axis_index("blk"), 2)
    copies = []
    for at, (back_ref, first) in enumerate(zip(backs, (2, odd))):
        for user in range(0, users, 2):
            both = back_ref[user * tasks : (user + 2) * tasks, :].astype(F32)
            held[at, user] = both[:tasks]
            held[at, user + 1] = both[tasks:]
        for k in range(2):
            place = out_ref.at[:, first + k * REACH]
            copies.append(pltpu.make_async_copy(held.at[at], place, sems.at[2 * at + k]))
            copies[-1].start()
    for copy in copies:
        copy.wait()


def shift(block, axis, distance):
    count = lax.axis_size(axis)
    return lax.ppermute(block, axis, [((i + distance) % count, i) for i in range(count)])


def spread(piece, shares, parts, own=False):
    row = [piece]
    for r in range(1, parts):
        row.append(shift(piece, "users", r))
    table = [row]
    for s in range(1, shares):
        line = [None]
        for r in range(parts):
            if r or not own or parts == 1:
                entry = shift(row[r], "sub", s)
                line[r:] = [entry]
        table.append(line)
    return table


def shards(
    history,
    lengths,
    item_rows,
    w_query,
    w_item,
    w_key,
    w_value,
    w_pooled,
    w_joint,
    bias_hidden,
    w_task,
    bias_task,
):
    users, tokens, width = history.shape
    items = item_rows.shape[0]
    hid, tasks = w_task.shape
    count, parts, shares = (lax.axis_size(axis) for axis in ("blk", "users", "sub"))
    full = tokens * parts

    share = users // shares
    piece = call(
        functools.partial(pack_kernel, shares),
        pltpu.VMEM((share * tokens + LENGTH_ROWS, width), BF16),
        [HBM] * 2,
        VMEM,
        (history, lengths),
        0,
        (pltpu.SMEM(lengths.shape, jnp.int32), pltpu.SemaphoreType.DMA((share + 1,))),
    )
    operands = (item_rows, w_query, w_item, w_joint, bias_hidden[None], w_task.T)
    mine, heads, bias = call(
        project_kernel,
        (
            pltpu.VMEM((width + hid, items), BF16),
            pltpu.VMEM((2 * tasks, 2 * hid), BF16),
            pltpu.VMEM((2 * tasks, 128), F32),
        ),
        [HBM] * 7,
        [VMEM] * 3,
        (*operands, bias_task),
        2 * items * item_rows.shape[1] * 2 * width,
        (
            *(pltpu.VMEM(a.shape, a.dtype) for a in operands),
            pltpu.SMEM(bias_task.shape, F32),
            pltpu.SemaphoreType.DMA((7,)),
        ),
    )
    flops = 2 * users * items * (full * (width + hid) + hid * tasks)
    state = (
        pltpu.VMEM((share * full, width), BF16),
        pltpu.VMEM((share // 2, 2 * hid, 2 * full + hid), BF16),
        pltpu.VMEM((share * full, 128), F32),
    )
    kept = pltpu.VMEM((users, tasks, items), F32)
    sent = pltpu.VMEM((users * tasks, items), BF16)
    rows = pltpu.VMEM((share * full, width), BF16)
    weights = (w_key, w_value, w_pooled)

    def scratch(turns):
        return (
            pltpu.VMEM((turns * share * full, items), F32),
            pltpu.VMEM((turns * share * full, items), BF16),
            pltpu.VMEM((turns * share // 2, 2 * hid, items), BF16),
        )

    def own_start(table):
        flat = [entry for row in table for entry in row if entry is not None]
        result, *states = call(
            functools.partial(own_kernel, shares, parts),
            (kept, *(state * shares)),
            [VMEM] * (len(flat) + 7),
            [VMEM] * (1 + 3 * shares),
            (history, *flat, *weights, mine, heads, bias),
            flops + 4 * users * full * width * width,
            (pltpu.VMEM((shares, share * full, width), BF16), *scratch(shares)),
        )
        return result, states

    def go_on(states, block, out):
        return call(
            functools.partial(next_kernel, shares, parts),
            out,
            [VMEM] * (len(states) + 3),
            VMEM,
            (block, *states, heads, bias),
            flops,
            scratch(shares),
        )

    if count != REACH or parts == 1:
        window = [None] * WIN
        window[REACH], held = own_start(spread(piece, shares, parts, True))
        low = high = mine
        for offset in range(1, REACH + 1):
            low, high = shift(low, "blk", -1), shift(high, "blk", 1)
            window[REACH - offset] = go_on(held, low, kept)
            window[REACH + offset] = go_on(held, high, kept)
        return jnp.stack(window, axis=1)

    across = [(i ^ 2, i) for i in range(count)]
    far = lax.ppermute(piece, "blk", across)
    other = lax.ppermute(mine, "blk", [(i ^ 1, i) for i in range(count)])
    table = spread(far, shares, parts)
    own = spread(piece, shares, parts, True)
    space = share * tokens
    early = call(
        early_kernel,
        (
            pltpu.VMEM((shares * space, width), BF16),
            pltpu.VMEM((shares * space, hid), F32),
            pltpu.VMEM((shares * space, items), F32),
        ),
        [VMEM] * (shares + 4),
        [VMEM] * 3,
        (*(line[0] for line in table), *weights, mine),
        flops // parts,
        (pltpu.VMEM((shares * space, width), BF16),),
    )
    ready, guests = [], []
    for s, line in enumerate(table):
        last = s == shares - 1
        result, *held = call(
            functools.partial(share_kernel, shares, parts, s),
            (sent if last else pltpu.VMEM((share * tasks, items), BF16), *state),
            [VMEM] * (parts + 8 + (s if last else 0)),
            [VMEM] * 4,
            (*line[1:], *early, *weights, mine, heads, bias, *(ready if last else ())),
            flops // shares,
            (pltpu.VMEM(((parts - 1) * space, width), BF16), *scratch(1)),
        )
        ready.append(result)
        guests += held
    first = lax.ppermute(result, "blk", across)
    result = go_on(guests, other, sent)
    second = lax.ppermute(result, "blk", across)
    at_home, held = own_start(own)
    beside = go_on(held, other, kept)
    whole = jax.ShapeDtypeStruct((users, WIN, tasks, items), F32)
    semaphores = pltpu.SemaphoreType.DMA((5,))
    out = call(place_own_kernel, whole, [VMEM] * 2, HBM, (at_home, beside), 0, (semaphores,))
    held = (pltpu.VMEM((2, users, tasks, items), F32), pltpu.SemaphoreType.DMA((4,)))
    specs = [VMEM, VMEM, HBM]
    return call(place_away_kernel, whole, specs, HBM, (first, second, out), 0, held, {2: 0})


def solution(mesh):
    placed = (
        P(("parts", "blk"), "users", None),
        P(("parts", "blk")),
        P(("parts", "blk", "users", "sub"), None),
        P(),
        P(),
        P(),
        P(),
        P(),
        P(),
        P(),
        P(),
        P(),
    )

    return jax.shard_map(
        shards,
        mesh=mesh,
        in_specs=placed,
        out_specs=P(("parts", "blk"), None, None, ("users", "sub")),
        check_vma=False,
    )
```

```python
import functools
import math

import jax
import jax.numpy as jnp
from jax import lax
from jax.experimental import pallas as pl
from jax.experimental.pallas import tpu as pltpu
from jax.sharding import PartitionSpec as P


REACH = 4
WIN = 2 * REACH + 1
LENGTH_ROWS = 8
KERNEL_BYTES = 16 << 20
BF16 = jnp.bfloat16
F32 = jnp.float32
VMEM = pl.BlockSpec(memory_space=pltpu.VMEM)
SMEM = pl.BlockSpec(memory_space=pltpu.SMEM)
HBM = pl.BlockSpec(memory_space=pltpu.HBM)


def call(kernel, out_shape, in_specs, out_specs, args, flops, scratch=(), aliases=None):
    moved = sum(math.prod(a.shape) * a.dtype.itemsize for a in args)
    spaces = {id(VMEM): pltpu.VMEM, id(HBM): pltpu.HBM}
    args = [pltpu.with_memory_space_constraint(a, spaces[id(spec)]) for a, spec in zip(args, in_specs)]
    return pl.pallas_call(
        kernel,
        out_shape=out_shape,
        in_specs=in_specs,
        out_specs=out_specs,
        scratch_shapes=list(scratch),
        input_output_aliases=aliases or {},
        compiler_params=pltpu.CompilerParams(vmem_limit_bytes=KERNEL_BYTES),
        cost_estimate=pl.CostEstimate(flops=flops, bytes_accessed=moved, transcendentals=0),
    )(*args)


def pack_kernel(shares, history_ref, lengths_ref, piece_ref, held_ref, sems):
    users, tokens, _ = history_ref.shape
    users //= shares
    width = piece_ref.shape[1]
    first = lax.axis_index("sub") * users
    copies = [pltpu.make_async_copy(lengths_ref, held_ref, sems.at[users])]
    for user in range(users):
        place = piece_ref.at[pl.ds(user * tokens, tokens)]
        copies.append(pltpu.make_async_copy(history_ref.at[first + user], place, sems.at[user]))
    for copy in copies:
        copy.start()
    copies[0].wait()
    row = lax.broadcasted_iota(jnp.int32, (LENGTH_ROWS, width), 0)
    lengths = jnp.zeros((LENGTH_ROWS, width), F32)
    for user in range(users):
        lengths = jnp.where(row == user, held_ref[first + user].astype(F32), lengths)
    piece_ref[users * tokens :, :] = lengths.astype(BF16)
    for copy in copies[1:]:
        copy.wait()


def project_kernel(*refs):
    sources, (out_ref, heads_ref, bias_out), held, sems = refs[:7], refs[7:10], refs[10:17], refs[17]
    copies = [pltpu.make_async_copy(*pair, sems.at[i]) for i, pair in enumerate(zip(sources, held))]
    for copy in copies:
        copy.start()
    items_ref, w_query_ref, w_item_ref, w_joint_ref, bias_ref, w_task_ref, bias_task_ref = held
    for copy in copies[5:]:
        copy.wait()
    tasks, hid = w_task_ref.shape
    w_task = w_task_ref[...].astype(F32)
    blank = jnp.zeros_like(w_task)
    heads_ref[:, :hid] = jnp.concatenate([w_task, blank], 0).astype(BF16)
    heads_ref[:, hid:] = jnp.concatenate([blank, w_task], 0).astype(BF16)
    row = lax.broadcasted_iota(jnp.int32, bias_out.shape, 0) % tasks
    bias = jnp.zeros(bias_out.shape, F32)
    for task in range(tasks):
        bias = jnp.where(row == task, bias_task_ref[task], bias)
    bias_out[...] = bias
    for copy in copies[:5]:
        copy.wait()
    width = w_query_ref.shape[1]
    rows = items_ref[...]
    queries = jnp.dot(rows, w_query_ref[...], preferred_element_type=F32)
    out_ref[:width, :] = queries.T.astype(BF16)
    joined = jnp.dot(rows, w_item_ref[...], preferred_element_type=F32).astype(BF16)
    terms = jnp.dot(joined, w_joint_ref[...], preferred_element_type=F32) + bias_ref[...]
    out_ref[width:, :] = terms.T.astype(BF16)


def project_tokens(rows_ref, weights):
    w_key_ref, w_value_ref, w_pooled_ref = weights
    keys = jnp.dot(rows_ref[...], w_key_ref[...], preferred_element_type=F32).astype(BF16)
    values = jnp.dot(rows_ref[...], w_value_ref[...], preferred_element_type=F32).astype(BF16)
    return keys, jnp.dot(values, w_pooled_ref[...], preferred_element_type=F32)


def arrange(pooled, firsts, lengths, state):
    _, pooled_ref, mask_ref = state
    pairs, hid, depth = pooled_ref.shape
    hid //= 2
    both = depth - hid
    full = both // 2
    parts = len(firsts)
    tokens = full // parts
    for r, first in enumerate(firsts):
        at = (lax.broadcasted_iota(jnp.int32, (tokens, 128), 0) + first).astype(F32)
        for user in range(2 * pairs):
            start = user * full + r * tokens
            valid = at < lengths[user : user + 1, :128]
            mask_ref[start : start + tokens, :] = jnp.where(valid, 0.0, -jnp.inf)
    lane = lax.broadcasted_iota(jnp.int32, (hid, both), 1)
    one = lax.broadcasted_iota(jnp.int32, (2 * hid, hid), 0) % hid
    one = jnp.where(one == lax.broadcasted_iota(jnp.int32, (2 * hid, hid), 1), 1.0, 0.0).astype(BF16)
    for pair in range(pairs):
        rows = [pooled(user, r) for user in (2 * pair, 2 * pair + 1) for r in range(parts)]
        flat = jnp.concatenate(rows, 0).T
        pooled_ref[pair, :hid, :both] = jnp.where(lane < full, flat, 0.0).astype(BF16)
        pooled_ref[pair, hid:, :both] = jnp.where(lane < full, 0.0, flat).astype(BF16)
        pooled_ref[pair, :, both:] = one


def score(items_ref, parts, states, heads_ref, bias_ref, scratch, put, late=None):
    scores_ref, weights_ref, hidden_ref = scratch
    width = states[0][0].shape[1]
    columns = items_ref.shape[1]
    factor = math.log2(math.e) / math.sqrt(width)
    bias = jnp.concatenate([bias_ref[...]] * (columns // 128), 1)
    count = states[0][0].shape[0]
    pairs, hid, depth = states[0][1].shape
    both = depth - hid // 2
    full = both // 2
    tokens = full // parts
    if late:
        early_ref, keys = late
    else:
        keys = jnp.concatenate([key_ref[...] for key_ref, _, _ in states], 0)
    scores = jnp.dot(keys, items_ref[:width, :], preferred_element_type=F32)
    scores_ref[: keys.shape[0], :] = scores
    for at, (_, _, mask_ref) in enumerate(states):
        for user in range(2 * pairs):
            rows = slice(user * full, (user + 1) * full)
            place = slice(at * count + user * full, at * count + (user + 1) * full)
            for column in range(0, columns, 128):
                lanes = slice(column, column + 128)
                if late:
                    found = [early_ref[user * tokens : (user + 1) * tokens, lanes]]
                    for r in range(parts - 1):
                        start = (r * 2 * pairs + user) * tokens
                        found.append(scores_ref[start : start + tokens, lanes])
                    scores = jnp.concatenate(found, 0)
                else:
                    scores = scores_ref[place, lanes]
                scores = scores + mask_ref[rows, :]
                maximum = jnp.max(scores, axis=0, keepdims=True)
                expo = jnp.exp2((scores - maximum) * factor)
                weights = expo * (1.0 / jnp.sum(expo, axis=0, keepdims=True))
                weights_ref[place, lanes] = weights.astype(BF16)
    turns = [(at, pair) for at in range(len(states)) for pair in range(pairs)]
    for at, pair in turns:
        start = at * count + pair * both
        inputs = jnp.concatenate([weights_ref[start : start + both, :], items_ref[width:, :]], 0)
        hidden = jnp.dot(states[at][1][pair], inputs, preferred_element_type=F32)
        hidden_ref[at * pairs + pair] = jnp.maximum(hidden, 0.0).astype(BF16)
    for at, pair in turns:
        hidden = hidden_ref[at * pairs + pair]
        put(at, pair, jnp.dot(heads_ref[...], hidden, preferred_element_type=F32) + bias)


def keep(out_ref, shares, pairs):
    tasks = out_ref.shape[1] if len(out_ref.shape) == 3 else None

    def put(share, pair, logits):
        user = 2 * (lax.rem(lax.axis_index("sub") + share, shares) * pairs + pair)
        count = logits.shape[0] // 2
        if tasks:
            out_ref[user] = logits[:count]
            out_ref[user + 1] = logits[count:]
        else:
            place = pl.multiple_of(user * count, 2 * count)
            out_ref[pl.ds(place, 2 * count), :] = logits.astype(out_ref.dtype)

    return put


def own_kernel(shares, parts, *refs):
    history_ref, *refs = refs
    given = shares * parts - (shares - 1 if parts > 1 else 0)
    pieces, refs = refs[:given], refs[given:]
    weights, (items_ref, heads_ref, bias_ref, out_ref), refs = refs[:3], refs[3:7], refs[7:]
    states = [tuple(refs[3 * s : 3 * s + 3]) for s in range(shares)]
    rows_ref, *scratch = refs[3 * shares :]
    side, me = lax.axis_index("sub"), lax.axis_index("users")
    users, tokens, width = history_ref.shape
    count = users // shares * tokens
    for s in range(shares):
        for r in range(parts):
            if s and not r and parts > 1:
                chosen = history_ref[pl.ds(lax.rem(side + s, shares) * (users // shares), users // shares)]
                rows = chosen.reshape(count, width)
            else:
                last = pieces.pop(0)
                rows = last[:count, :]
            for user in range(users // shares):
                start = (user * parts + r) * tokens
                rows_ref[s, start : start + tokens, :] = rows[user * tokens : (user + 1) * tokens]
        lengths = last[count:, :].astype(F32)
        keys, values = project_tokens(rows_ref.at[s], weights)
        states[s][0][...] = keys

        def pooled(user, r):
            start = (user * parts + r) * tokens
            return values[start : start + tokens]

        arrange(pooled, [lax.rem(me + r, parts) * tokens for r in range(parts)], lengths, states[s])
    put = keep(out_ref, shares, states[0][1].shape[0])
    score(items_ref, parts, states, heads_ref, bias_ref, scratch, put)


def early_kernel(shares, *refs):
    pieces, weights, blocks, refs = refs[:shares], refs[shares : shares + 3], refs[shares + 3 : 2 * shares + 3], refs[2 * shares + 3 :]
    key_ref, values_ref, scores_ref, rows_ref = refs
    count = rows_ref.shape[0] // shares
    for s, ref in enumerate(pieces):
        rows_ref[s * count : (s + 1) * count, :] = ref[:count, :]
    keys, values = project_tokens(rows_ref, weights)
    key_ref[...] = keys
    values_ref[...] = values
    queries = jnp.concatenate([ref[: keys.shape[1], :] for ref in blocks], 1)
    scores_ref[...] = jnp.dot(keys[:count], queries, preferred_element_type=F32)


def complete(parts, share, late, early, weights, state, rows_ref):
    me = lax.axis_index("users")
    count = rows_ref.shape[0] // (parts - 1)
    pairs = state[1].shape[0]
    tokens = count // (2 * pairs)
    for r, ref in enumerate(late):
        rows_ref[r * count : (r + 1) * count, :] = ref[:count, :]
    lengths = late[-1][count:, :].astype(F32)
    keys, values = project_tokens(rows_ref, weights)
    for user in range(2 * pairs):
        start = user * parts * tokens
        first = share * count + user * tokens
        state[0][start : start + tokens, :] = early[0][first : first + tokens, :]
        for r in range(parts - 1):
            start += tokens
            first = (r * 2 * pairs + user) * tokens
            state[0][start : start + tokens, :] = keys[first : first + tokens]

    def pooled(user, r):
        if r == 0:
            start = share * count + user * tokens
            return early[1][start : start + tokens, :]
        start = ((r - 1) * 2 * pairs + user) * tokens
        return values[start : start + tokens]

    arrange(pooled, [lax.rem(me + r, parts) * tokens for r in range(parts)], lengths, state)
    return keys


def far_kernel(shares, parts, *refs):
    late, early, refs = refs[: parts - 1], refs[parts - 1 : parts + 2], refs[parts + 2 :]
    weights, blocks, refs = refs[:3], refs[3 : shares + 3], refs[shares + 3 :]
    heads_ref, bias_ref, out_ref = refs[:3]
    state, rows_ref, scratch = tuple(refs[3:6]), refs[6], refs[7:]
    keys = complete(parts, 0, late, early, weights, state, rows_ref)
    items = out_ref.shape[1]

    def put(_, pair, logits):
        size = logits.shape[0]
        for s in range(shares):
            start = s * out_ref.shape[0] // shares + pair * size
            part = logits[:, s * items : (s + 1) * items]
            out_ref[start : start + size, :] = part.astype(out_ref.dtype)

    queries = jnp.concatenate([ref[...] for ref in blocks], 1)
    score(queries, parts, (state,), heads_ref, bias_ref, scratch, put, (early[2], keys))


def far_next_kernel(shares, parts, *refs):
    count = (shares - 1) * (parts - 1)
    late, early, refs = refs[:count], refs[count : count + 2], refs[count + 2 :]
    states, weights, refs = [tuple(refs[:3])], refs[3:6], refs[6:]
    items_ref, heads_ref, bias_ref, out_ref, *refs = refs
    scratch, refs = refs[:3], refs[3:]
    for s in range(1, shares):
        state, rows_ref = tuple(refs[4 * s - 4 : 4 * s - 1]), refs[4 * s - 1]
        pieces = late[(s - 1) * (parts - 1) : s * (parts - 1)]
        complete(parts, s, pieces, early, weights, state, rows_ref)
        states.append(state)
    put = keep(out_ref, shares, states[0][1].shape[0])
    score(items_ref, parts, states, heads_ref, bias_ref, scratch, put)


def next_kernel(shares, parts, items_ref, *refs):
    states = [tuple(refs[3 * s : 3 * s + 3]) for s in range(shares)]
    heads_ref, bias_ref, out_ref, *scratch = refs[3 * shares :]
    put = keep(out_ref, shares, states[0][1].shape[0])
    score(items_ref, parts, states, heads_ref, bias_ref, scratch, put)


def place_own_kernel(home_ref, beside_ref, out_ref, sems):
    even = lax.rem(lax.axis_index("blk"), 2)
    places = [(home_ref, k) for k in range(0, WIN, REACH)]
    places += [(beside_ref, 1 + 2 * even), (beside_ref, 1 + 2 * even + REACH)]
    copies = [pltpu.make_async_copy(a, out_ref.at[:, k], sems.at[i]) for i, (a, k) in enumerate(places)]
    for copy in copies:
        copy.start()
    for copy in copies:
        copy.wait()


def place_away_kernel(shares, *refs):
    firsts, (second_ref, _, out_ref, held, sems) = refs[:shares], refs[shares:]
    _, users, tasks, _ = held.shape
    odd = 3 - 2 * lax.rem(lax.axis_index("blk"), 2)
    side = lax.axis_index("sub")
    share = users // shares
    copies = []
    for at, first in enumerate((2, odd)):
        for user in range(0, users, 2):
            if at:
                both = second_ref[user * tasks : (user + 2) * tasks, :].astype(F32)
                place = user
            else:
                s, u = user // share, user % share
                both = firsts[s][user * tasks : (user + 2) * tasks, :].astype(F32)
                place = lax.rem(side + shares - s, shares) * share + u
            held[at, place] = both[:tasks]
            held[at, place + 1] = both[tasks:]
        for k in range(2):
            target = out_ref.at[:, first + k * REACH]
            copies.append(pltpu.make_async_copy(held.at[at], target, sems.at[2 * at + k]))
            copies[-1].start()
    for copy in copies:
        copy.wait()


def shift(block, axis, distance):
    count = lax.axis_size(axis)
    return lax.ppermute(block, axis, [((i + distance) % count, i) for i in range(count)])


def spread(piece, shares, parts, own=False):
    row = [piece]
    for r in range(1, parts):
        row.append(shift(piece, "users", r))
    table = [row]
    for s in range(1, shares):
        line = [None]
        for r in range(parts):
            if r or not own or parts == 1:
                entry = shift(row[r], "sub", s)
                line[r:] = [entry]
        table.append(line)
    return table


def shards(
    history,
    lengths,
    item_rows,
    w_query,
    w_item,
    w_key,
    w_value,
    w_pooled,
    w_joint,
    bias_hidden,
    w_task,
    bias_task,
):
    users, tokens, width = history.shape
    items = item_rows.shape[0]
    hid, tasks = w_task.shape
    count, parts, shares = (lax.axis_size(axis) for axis in ("blk", "users", "sub"))
    full = tokens * parts

    share = users // shares
    piece = call(
        functools.partial(pack_kernel, shares),
        pltpu.VMEM((share * tokens + LENGTH_ROWS, width), BF16),
        [HBM] * 2,
        VMEM,
        (history, lengths),
        0,
        (pltpu.SMEM(lengths.shape, jnp.int32), pltpu.SemaphoreType.DMA((share + 1,))),
    )
    operands = (item_rows, w_query, w_item, w_joint, bias_hidden[None], w_task.T)
    mine, heads, bias = call(
        project_kernel,
        (
            pltpu.VMEM((width + hid, items), BF16),
            pltpu.VMEM((2 * tasks, 2 * hid), BF16),
            pltpu.VMEM((2 * tasks, 128), F32),
        ),
        [HBM] * 7,
        [VMEM] * 3,
        (*operands, bias_task),
        2 * items * item_rows.shape[1] * 2 * width,
        (
            *(pltpu.VMEM(a.shape, a.dtype) for a in operands),
            pltpu.SMEM(bias_task.shape, F32),
            pltpu.SemaphoreType.DMA((7,)),
        ),
    )
    flops = 2 * users * items * (full * (width + hid) + hid * tasks)
    state = (
        pltpu.VMEM((share * full, width), BF16),
        pltpu.VMEM((share // 2, 2 * hid, 2 * full + hid), BF16),
        pltpu.VMEM((share * full, 128), F32),
    )
    kept = pltpu.VMEM((users, tasks, items), F32)
    sent = pltpu.VMEM((users * tasks, items), BF16)
    rows = pltpu.VMEM((share * full, width), BF16)
    weights = (w_key, w_value, w_pooled)

    def scratch(turns):
        return (
            pltpu.VMEM((turns * share * full, items), F32),
            pltpu.VMEM((turns * share * full, items), BF16),
            pltpu.VMEM((turns * share // 2, 2 * hid, items), BF16),
        )

    def own_start(table):
        flat = [entry for row in table for entry in row if entry is not None]
        result, *states = call(
            functools.partial(own_kernel, shares, parts),
            (kept, *(state * shares)),
            [VMEM] * (len(flat) + 7),
            [VMEM] * (1 + 3 * shares),
            (history, *flat, *weights, mine, heads, bias),
            flops + 4 * users * full * width * width,
            (pltpu.VMEM((shares, share * full, width), BF16), *scratch(shares)),
        )
        return result, states

    def go_on(states, block, out):
        return call(
            functools.partial(next_kernel, shares, parts),
            out,
            [VMEM] * (len(states) + 3),
            VMEM,
            (block, *states, heads, bias),
            flops,
            scratch(shares),
        )

    if count != REACH or parts == 1:
        window = [None] * WIN
        window[REACH], held = own_start(spread(piece, shares, parts, True))
        low = high = mine
        for offset in range(1, REACH + 1):
            low, high = shift(low, "blk", -1), shift(high, "blk", 1)
            window[REACH - offset] = go_on(held, low, kept)
            window[REACH + offset] = go_on(held, high, kept)
        return jnp.stack(window, axis=1)

    across = [(i ^ 2, i) for i in range(count)]
    far = lax.ppermute(piece, "blk", across)
    other = lax.ppermute(mine, "blk", [(i ^ 1, i) for i in range(count)])
    blocks = [mine]
    for turn in range(1, shares):
        blocks.append(shift(mine, "sub", turn))
    table = spread(far, shares, parts)
    own = spread(piece, shares, parts, True)
    space = share * tokens
    late_rows = pltpu.VMEM(((parts - 1) * space, width), BF16)
    early = call(
        functools.partial(early_kernel, shares),
        (
            pltpu.VMEM((shares * space, width), BF16),
            pltpu.VMEM((shares * space, hid), F32),
            pltpu.VMEM((space, shares * items), F32),
        ),
        [VMEM] * (2 * shares + 3),
        [VMEM] * 3,
        (*(line[0] for line in table), *weights, *blocks),
        flops // parts,
        (pltpu.VMEM((shares * space, width), BF16),),
    )
    result, *guests = call(
        functools.partial(far_kernel, shares, parts),
        (sent, *state),
        [VMEM] * (parts + 7 + shares),
        [VMEM] * 4,
        (*table[0][1:], *early, *weights, *blocks, heads, bias),
        flops,
        (
            late_rows,
            pltpu.VMEM(((parts - 1) * space, shares * items), F32),
            pltpu.VMEM((share * full, shares * items), BF16),
            pltpu.VMEM((share // 2, 2 * hid, shares * items), BF16),
        ),
    )
    firsts = [lax.ppermute(result, "blk", across)]
    for turn in range(1, shares):
        firsts.append(shift(firsts[0], "sub", -turn))
    late = [entry for line in table[1:] for entry in line[1:]]
    result = call(
        functools.partial(far_next_kernel, shares, parts),
        sent,
        [VMEM] * (len(late) + 11),
        VMEM,
        (*late, *early[:2], *guests, *weights, other, heads, bias),
        flops,
        (*scratch(shares), *((*state, late_rows) * (shares - 1))),
    )
    second = lax.ppermute(result, "blk", across)
    at_home, held = own_start(own)
    beside = go_on(held, other, kept)
    whole = jax.ShapeDtypeStruct((users, WIN, tasks, items), F32)
    semaphores = pltpu.SemaphoreType.DMA((5,))
    out = call(place_own_kernel, whole, [VMEM] * 2, HBM, (at_home, beside), 0, (semaphores,))
    held = (pltpu.VMEM((2, users, tasks, items), F32), pltpu.SemaphoreType.DMA((4,)))
    specs = [VMEM] * (shares + 1) + [HBM]
    kernel = functools.partial(place_away_kernel, shares)
    return call(kernel, whole, specs, HBM, (*firsts, second, out), 0, held, {shares + 1: 0})


def solution(mesh):
    placed = (
        P(("parts", "blk"), "users", None),
        P(("parts", "blk")),
        P(("parts", "blk", "users", "sub"), None),
        P(),
        P(),
        P(),
        P(),
        P(),
        P(),
        P(),
        P(),
        P(),
    )

    return jax.shard_map(
        shards,
        mesh=mesh,
        in_specs=placed,
        out_specs=P(("parts", "blk"), None, None, ("users", "sub")),
        check_vma=False,
    )
```
